128 devices in a mesh: section: 8 (over x, core), tensor: 16 (over z, y).
Axes of the slice: x: 4, y: 4, z: 4, core: 2. Of those that a mesh axis runs over, the one named last changes fastest.
Arguments:
- hidden_in: bfloat16 [64, 2560], P(None, 'tensor'), may hold values from -6 to 6
- pre_gain: float32 [8, 2560], P('section'), may hold values from 0.1 to 1.9
- w_zx: bfloat16 [8, 2560, 80, 128], P('section', None, 'tensor'), may hold values from -0.125 to 0.125
- w_bc: bfloat16 [8, 2560, 256], P('section'), may hold values from -0.125 to 0.125
- w_dt: bfloat16 [8, 2560, 80], P('section', None, 'tensor'), may hold values from -0.125 to 0.125
- dt_bias: float32 [8, 80], P('section', 'tensor'), may hold values from -4 to -1
- a_log: float32 [8, 80], P('section', 'tensor'), may hold values from 0 to 2.77
- d_skip: float32 [8, 80], P('section', 'tensor'), may hold values from 0.5 to 2
- conv_x_weight: float32 [8, 4, 80, 64], P('section', None, 'tensor'), may hold values from -3 to 3
- conv_x_bias: float32 [8, 80, 64], P('section', 'tensor'), may hold values from -3 to 3
- conv_bc_weight: float32 [8, 4, 256], P('section'), may hold values from -3 to 3
- conv_bc_bias: float32 [8, 256], P('section'), may hold values from -3 to 3
- inner_gain: float32 [8, 80, 64], P('section', 'tensor'), may hold values from 0.1 to 1.9
- w_out: bfloat16 [8, 80, 64, 2560], P('section', 'tensor'), may hold values from -0.078125 to 0.078125
- conv_x_state: bfloat16 [8, 64, 3, 80, 64], P('section', None, None, 'tensor'), may hold values from -6 to 6
- conv_bc_state: bfloat16 [8, 64, 3, 256], P('section'), may hold values from -6 to 6
- ssm_state: bfloat16 [8, 64, 80, 64, 128], P('section', None, 'tensor'), may hold values from -14 to 14
Outputs:
- section_hidden: bfloat16 [8, 64, 2560], P('section', None, 'tensor')
- conv_x_new: bfloat16 [8, 64, 3, 80, 64], P('section', None, None, 'tensor')
- conv_bc_new: bfloat16 [8, 64, 3, 256], P('section')
- ssm_new: bfloat16 [8, 64, 80, 64, 128], P('section', None, 'tensor')
The draws below stay inside these ranges and needn't reach their ends.
All inputs are finite; a program needn't handle non-finite values.
Results may differ from the reference program's by a relative error of at most 0.02.
Values may be sent and summed in bfloat16 or wider, within the bound.
A program may use at most 64 MiB of HBM per device.

```python
import jax
import jax.numpy as jnp
from jax import lax

D = 2560
H = 80
P_SIZE = 64
N = 128
K = 4
L_DEV = 1
STREAMS = 64
LAYERS = 8


def draw_ssm_state(key, part):
    heads = jnp.arange(H, dtype=jnp.float32) / (H - 1)
    scales = 0.5 * 8.0 ** heads
    values = jnp.clip(jax.random.normal(key, (LAYERS, STREAMS, H, P_SIZE, N), jnp.float32), -3.5, 3.5)
    return (values * scales[None, None, :, None, None]).astype(jnp.bfloat16)


def block_scale(rng, extent, pieces, smallest, largest):
    level = 1.0
    for axis_at, parts in pieces:
        draws = jax.random.uniform(jax.random.fold_in(jax.random.fold_in(rng, 6), axis_at), (parts,), jnp.float32, smallest / len(pieces), largest / len(pieces))
        level = level * jnp.repeat(jnp.exp(draws), extent[axis_at] // parts).reshape((-1,) + (1,) * (len(extent) - 1 - axis_at))
    return level


def centred(own_key, shape, scale, bound, cuts=(), kind=jnp.bfloat16):
    values = jax.random.normal(own_key, shape, jnp.float32) * scale
    if len(cuts) > 0:
        values = block_scale(own_key, shape, cuts, -0.22, 0.18) * values
    return jnp.clip(values, min=-bound, max=bound).astype(kind)


def setup_inputs(seed: int = 0) -> dict:
    key_of = jax.random.split(jax.random.key(seed), 18)
    hidden_in = centred(key_of[0], (STREAMS, D), 1.0, 6.0, ((1, 16),))
    pre_gain = jnp.clip(1.0 + 0.18 * jax.random.normal(key_of[1], (LAYERS, D), jnp.float32), 0.1, 1.9)
    w_zx = centred(key_of[2], (LAYERS, D, H, 2 * P_SIZE), D ** -0.5, 0.125, ((0, 8), (2, 16)))
    w_bc = centred(key_of[3], (LAYERS, D, 2 * N), D ** -0.5, 0.125, ((0, 8),))
    w_dt = centred(key_of[4], (LAYERS, D, H), D ** -0.5, 0.125, ((0, 8), (2, 16)))
    dt_bias = jnp.clip(-4.0 + 3.0 * jax.random.uniform(key_of[5], (LAYERS, H), jnp.float32) ** block_scale(key_of[5], (LAYERS, H), ((0, 8), (1, 16)), -0.2, 0.2), -4.0, -1.0)
    a_log = jnp.clip(2.77 * jax.random.uniform(key_of[6], (LAYERS, H), jnp.float32) ** block_scale(key_of[6], (LAYERS, H), ((0, 8), (1, 16)), -0.2, 0.2), 0.0, 2.77)
    d_skip = jnp.clip(0.5 + 1.5 * jax.random.uniform(key_of[7], (LAYERS, H), jnp.float32) ** block_scale(key_of[7], (LAYERS, H), ((0, 8), (1, 16)), -0.2, 0.2), 0.5, 2.0)
    conv_x_weight = centred(key_of[8], (LAYERS, K, H, P_SIZE), K ** -0.5, 3.0, ((0, 8), (2, 16)), jnp.float32)
    conv_x_bias = centred(key_of[9], (LAYERS, H, P_SIZE), 0.5, 3.0, ((0, 8), (1, 16)), jnp.float32)
    conv_bc_weight = centred(key_of[10], (LAYERS, K, 2 * N), K ** -0.5, 3.0, ((0, 8),), jnp.float32)
    conv_bc_bias = centred(key_of[11], (LAYERS, 2 * N), 0.5, 3.0, ((0, 8),), jnp.float32)
    inner_gain = jnp.clip(1.0 + 0.18 * jax.random.normal(key_of[12], (LAYERS, H, P_SIZE), jnp.float32), 0.1, 1.9)
    w_out = centred(key_of[13], (LAYERS, H, P_SIZE, D), (H * P_SIZE) ** -0.5, 0.078125, ((0, 8), (1, 16)))
    conv_x_state = centred(key_of[14], (LAYERS, STREAMS, K - 1, H, P_SIZE), 1.0, 6.0, ((0, 8), (3, 16)))
    conv_bc_state = centred(key_of[15], (LAYERS, STREAMS, K - 1, 2 * N), 1.0, 6.0, ((0, 8),))
    ssm_state = draw_ssm_state(jax.random.fold_in(key_of[17], 71), 0)
    return {"hidden_in": hidden_in, "pre_gain": pre_gain, "w_zx": w_zx, "w_bc": w_bc, "w_dt": w_dt, "dt_bias": dt_bias, "a_log": a_log, "d_skip": d_skip, "conv_x_weight": conv_x_weight, "conv_x_bias": conv_x_bias, "conv_bc_weight": conv_bc_weight, "conv_bc_bias": conv_bc_bias, "inner_gain": inner_gain, "w_out": w_out, "conv_x_state": conv_x_state, "conv_bc_state": conv_bc_state, "ssm_state": ssm_state}


epsilon = 1e-05

def mixer_core(normed, w_zx, w_bc, w_dt, dt_bias, a_log, d_skip, conv_x_weight, conv_x_bias, conv_bc_weight, conv_bc_bias, conv_x_state, conv_bc_state, ssm_state):
    row_count = normed.shape[0]
    model_width = w_zx.shape[0]
    head_count = w_zx.shape[1]
    head_size = w_zx.shape[2] // 2
    state_size = w_bc.shape[1] // 2
    both_parts = jnp.dot(normed, w_zx.reshape(model_width, head_count * 2 * head_size), preferred_element_type=jnp.float32)
    both_parts = both_parts.reshape(row_count, head_count, 2 * head_size)
    gate_z = both_parts[:, :, :head_size]
    x_fresh = both_parts[:, :, head_size:].astype(jnp.bfloat16)
    bc_fresh = jnp.dot(normed, w_bc, preferred_element_type=jnp.float32).astype(jnp.bfloat16)
    dt_raw = jnp.dot(normed, w_dt, preferred_element_type=jnp.float32)
    x_window = jnp.concatenate([conv_x_state, x_fresh[:, None]], axis=1)
    bc_window = jnp.concatenate([conv_bc_state, bc_fresh[:, None]], axis=1)
    x_conv = jax.nn.silu(lax.optimization_barrier(jnp.sum(x_window.astype(jnp.float32) * conv_x_weight[None], axis=1)) + conv_x_bias[None])
    bc_conv = jax.nn.silu(lax.optimization_barrier(jnp.sum(bc_window.astype(jnp.float32) * conv_bc_weight[None], axis=1)) + conv_bc_bias[None])
    b_input = bc_conv[:, :state_size]
    c_output = bc_conv[:, state_size:]
    step_size = jax.nn.softplus(dt_raw + dt_bias[None])
    decay_rate = jnp.exp(-step_size * jnp.exp(a_log)[None])
    state_f = decay_rate[:, :, None, None] * ssm_state.astype(jnp.float32) + (step_size[:, :, None] * x_conv)[:, :, :, None] * b_input[:, None, None, :]
    y_out = lax.optimization_barrier(jnp.sum(state_f * c_output[:, None, None, :], axis=-1)) + d_skip[None, :, None] * x_conv
    gated_out = y_out * jax.nn.silu(gate_z)
    return (gated_out, x_window[:, 1:], bc_window[:, 1:], state_f.astype(jnp.bfloat16))

def reference(hidden_in, pre_gain, w_zx, w_bc, w_dt, dt_bias, a_log, d_skip, conv_x_weight, conv_x_bias, conv_bc_weight, conv_bc_bias, inner_gain, w_out, conv_x_state, conv_bc_state, ssm_state):
    hidden = hidden_in
    section_list = []
    conv_x_list = []
    conv_bc_list = []
    ssm_list = []
    for which_layer in range(LAYERS):
        wide = hidden.astype(jnp.float32)
        normed = (wide * lax.rsqrt(lax.optimization_barrier(jnp.mean(wide * wide, axis=-1, keepdims=True)) + epsilon) * pre_gain[which_layer][None]).astype(jnp.bfloat16)
        gated_out, conv_x_next, conv_bc_next, ssm_next = mixer_core(normed, w_zx[which_layer], w_bc[which_layer], w_dt[which_layer], dt_bias[which_layer], a_log[which_layer], d_skip[which_layer], conv_x_weight[which_layer], conv_x_bias[which_layer], conv_bc_weight[which_layer], conv_bc_bias[which_layer], conv_x_state[which_layer], conv_bc_state[which_layer], ssm_state[which_layer])
        squares = lax.optimization_barrier(jnp.mean(gated_out * gated_out, axis=(1, 2)))
        scaled_inner = (gated_out * inner_gain[which_layer][None]).astype(jnp.bfloat16)
        head_count = scaled_inner.shape[1]
        head_size = scaled_inner.shape[2]
        product = jnp.dot(scaled_inner.reshape(scaled_inner.shape[0], head_count * head_size), w_out[which_layer].reshape(head_count * head_size, w_out.shape[-1]), preferred_element_type=jnp.float32)
        mixed = product * lax.rsqrt(squares + epsilon)[:, None]
        hidden = (wide + mixed).astype(jnp.bfloat16)
        conv_x_list.append(conv_x_next)
        conv_bc_list.append(conv_bc_next)
        ssm_list.append(ssm_next)
        if (which_layer + 1) % L_DEV == 0:
            section_list.append(hidden)
    return (jnp.stack(section_list), jnp.stack(conv_x_list), jnp.stack(conv_bc_list), jnp.stack(ssm_list))
```

```python
import functools

import jax
import jax.numpy as jnp
from jax import lax
from jax.experimental import pallas as pl
from jax.experimental.pallas import tpu as pltpu
from jax.sharding import PartitionSpec as P

epsilon = 1e-05
MESH = pl.DeviceIdType.MESH
F32, BF16 = jnp.float32, jnp.bfloat16
SIDE = 4
NEAR = (0, 1, 3, 2)
FAR = (2, 1, 3, 0)


def silu(v):
    return v / (1.0 + jnp.exp(-v))


def softplus(v):
    return jnp.maximum(v, 0.0) + jnp.log1p(jnp.exp(-jnp.abs(v)))


def kernel(
    sections,
    hid_ref,
    gain_ref,
    wzx_hbm,
    wbc_hbm,
    wdt_ref,
    dtb_ref,
    alog_ref,
    dsk_ref,
    cxw_ref,
    cxb_ref,
    cbw_ref,
    cbb_ref,
    ig_ref,
    wout_hbm,
    cxs_ref,
    cbs_ref,
    ssm_hbm,
    sec_out,
    cx_out,
    cb_out,
    ssm_out,
    w_all,
    w_o,
    st,
    hbuf,
    acc,
    wdt_pad,
    pre_bc,
    pre_x,
    par,
    q_buf,
    inner,
    stx,
    dec,
    b_buf,
    xf_buf,
    stx_t,
    dec_t,
    send_buf,
    rs_buf,
    ag_src,
    init_buf,
    sh_buf,
    load_sem,
    out_sem,
    init_send,
    init_recv,
    rs_send,
    rs_recv,
    ag_send,
    ag_recv,
    sh_send,
    sh_recv,
):
    heads, streams, p_size = cxs_ref.shape[1:]
    width, n2 = wbc_hbm.shape
    n_state = n2 // 2
    chunk = width // SIDE
    rows = streams // SIDE
    share = hid_ref.shape[1]
    team = SIDE * SIDE
    last = sections - 1

    sec = lax.axis_index("section")
    me = lax.axis_index("tensor")
    my_z = me // SIDE
    my_y = me % SIDE

    def dev(s, t):
        return {"section": s, "tensor": t}

    loads = [pltpu.make_async_copy(wbc_hbm, w_all.at[:, pl.ds(0, n2)], load_sem.at[0])]
    for h in range(heads):
        loads.append(
            pltpu.make_async_copy(
                wzx_hbm.at[h], w_all.at[:, pl.ds(n2 + 128 * h, 128)], load_sem.at[1 + h]
            )
        )
    at = 1 + heads
    for yy in range(SIDE):
        loads.append(
            pltpu.make_async_copy(
                wout_hbm.at[:, pl.ds(chunk * yy, chunk)], w_o.at[yy], load_sem.at[at + yy]
            )
        )
    at += SIDE
    loads.append(pltpu.make_async_copy(ssm_hbm, st, load_sem.at[at]))

    barrier = pltpu.get_barrier_semaphore()

    def greet(j, carry):
        other = (me + j) % team

        @pl.when(j > 0)
        def _():
            pl.semaphore_signal(barrier, inc=1, device_id=dev(sec, other), device_id_type=MESH)

        @pl.when(sec > 0)
        def _():
            pl.semaphore_signal(barrier, inc=1, device_id=dev(sec - 1, other), device_id_type=MESH)

        @pl.when(sec < last)
        def _():
            pl.semaphore_signal(barrier, inc=1, device_id=dev(sec + 1, other), device_id_type=MESH)

        return carry

    lax.fori_loop(0, team, greet, 0)
    for cp in loads:
        cp.start()
    partners = team - 1 + jnp.where(sec > 0, team, 0) + jnp.where(sec < last, team, 0)
    pl.semaphore_wait(barrier, partners)

    def init_copy(dest):
        return pltpu.make_async_remote_copy(
            src_ref=hid_ref,
            dst_ref=init_buf.at[me],
            send_sem=init_send.at[dest],
            recv_sem=init_recv.at[me],
            device_id=dev(sec, dest),
            device_id_type=MESH,
        )

    def init_own():
        return pltpu.make_async_copy(hid_ref, init_buf.at[me], init_recv.at[me])

    @pl.when(sec == 0)
    def _():
        def go(j, carry):
            init_copy((me + j) % team).start()
            return carry

        lax.fori_loop(1, team, go, 0)
        init_own().start()

    lane = lax.broadcasted_iota(jnp.int32, (streams, 128), 1)
    low = lane < p_size
    wdt_pad[...] = jnp.zeros_like(wdt_pad)
    wdt_pad[0:heads, :] = wdt_ref[...].astype(F32)
    for h in range(1 + heads):
        loads[h].wait()
    for j in range(width // 128):
        blk = wdt_pad[:, 128 * j : 128 * j + 128]
        w_all[128 * j : 128 * j + 128, n2 + 128 * heads : n2 + 128 * heads + 128] = blk.T.astype(BF16)
    acc[...] = jnp.zeros_like(acc)
    q_buf[...] = jnp.zeros_like(q_buf)
    cbw = cbw_ref[...]
    pre_bc[...] = (
        cbs_ref[0].astype(F32) * cbw[0:1]
        + cbs_ref[1].astype(F32) * cbw[1:2]
        + cbs_ref[2].astype(F32) * cbw[2:3]
        + cbb_ref[...]
    )
    pairs = (heads + 1) // 2

    def packed(get, k):
        a = get(2 * k)
        b = get(2 * k + 1) if 2 * k + 1 < heads else jnp.zeros_like(a)
        return jnp.concatenate([a, b], axis=1)

    def pre_of(h):
        w = cxw_ref[h]
        return (
            cxs_ref[0, h].astype(F32) * w[0:1]
            + cxs_ref[1, h].astype(F32) * w[1:2]
            + cxs_ref[2, h].astype(F32) * w[2:3]
            + cxb_ref[h]
        )

    for k in range(pairs):
        pre_x[k] = packed(pre_of, k)
        par[0, k] = packed(lambda h: cxw_ref[h][3:4], k)
        par[1, k] = packed(lambda h: ig_ref[h], k)
        par[2, k] = packed(
            lambda h: jnp.broadcast_to(dsk_ref[:, h : h + 1], (1, p_size)), k
        )
    pad = jnp.zeros((1, 128 - heads), F32)
    dtb = jnp.concatenate([dtb_ref[...], pad], axis=1)
    neg_a = -jnp.exp(jnp.concatenate([alog_ref[...], pad], axis=1))

    @pl.when(sec == 0)
    def _():
        def wait_one(k, carry):
            pltpu.make_async_copy(hid_ref, init_buf.at[k], init_recv.at[k]).wait()
            return carry

        lax.fori_loop(0, team, wait_one, 0)
        for yy in range(SIDE):
            parts = [init_buf[SIDE * yy + i].astype(F32) for i in range(SIDE)]
            hbuf[yy] = jnp.concatenate(parts, axis=1).astype(BF16)

    def ag_copy(src_t, dest):
        return pltpu.make_async_remote_copy(
            src_ref=ag_src,
            dst_ref=hbuf.at[src_t % SIDE, pl.ds(pl.multiple_of((src_t // SIDE) * rows, rows), rows), :],
            send_sem=ag_send.at[dest],
            recv_sem=ag_recv.at[src_t],
            device_id=dev(jnp.minimum(sec + 1, last), dest),
            device_id_type=MESH,
        )

    sq = jnp.zeros((streams, 128), F32)
    for off in NEAR:
        yy = (my_y + off) % SIDE

        @pl.when(sec > 0)
        def _():
            for zo in NEAR:
                ag_copy(((my_z + zo) % SIDE) * SIDE + yy, me).wait_recv()

        hv = hbuf[yy].astype(F32)
        for i in range(chunk // 128):
            part = hv[:, 128 * i : 128 * i + 128]
            sq = sq + part * part
        start = pl.multiple_of(yy * chunk, chunk)
        hg = (hv * gain_ref[:, pl.ds(start, chunk)]).astype(BF16)
        acc[...] += jnp.dot(hg, w_all[pl.ds(start, chunk), :], preferred_element_type=F32)
    r = lax.rsqrt(jnp.sum(sq, axis=1, keepdims=True) * (1.0 / width) + epsilon)

    bcf = (acc[:, 0:n2] * r).astype(BF16)
    cb_out[0] = cbs_ref[1]
    cb_out[1] = cbs_ref[2]
    cb_out[2] = bcf
    bcv = silu(pre_bc[...] + bcf.astype(F32) * cbw[3:4])
    b_in = bcv[:, 0:n_state]
    c_out = bcv[:, n_state:n2]
    b_buf[...] = b_in
    bd = jnp.sum(b_in * c_out, axis=1, keepdims=True)
    c_bf = c_out

    loads[-1].wait()
    group = 16
    row = lax.broadcasted_iota(jnp.int32, (group, n_state), 0)
    for g in range(streams // group):
        c16 = c_bf[group * g : group * g + group]
        total = None
        for i in range(0, group, 2):
            lhs = jnp.concatenate(
                [jnp.where(row == i, c16, 0.0), jnp.where(row == i + 1, c16, 0.0)], axis=1
            ).astype(BF16)
            rhs = jnp.concatenate([st[group * g + i], st[group * g + i + 1]], axis=1)
            term = lax.dot_general(
                lhs, rhs, (((1,), (1,)), ((), ())), preferred_element_type=F32
            )
            total = term if total is None else total + term
        q_buf[group * g : group * g + group, 0 : heads * p_size] = total

    dt0 = n2 + 128 * heads
    step = softplus(acc[:, dt0 : dt0 + 128] * r + dtb)
    decay = jnp.exp(step * neg_a)

    def spread(v, k):
        hi = min(2 * k + 1, heads - 1)
        a = jnp.broadcast_to(v[:, 2 * k : 2 * k + 1], (streams, 128))
        b = jnp.broadcast_to(v[:, hi : hi + 1], (streams, 128))
        return jnp.where(low, a, b)

    sq = jnp.zeros((streams, 128), F32)
    for k in range(pairs):
        a = acc[:, n2 + 256 * k : n2 + 256 * k + 128]
        if 2 * k + 1 < heads:
            b = acc[:, n2 + 256 * k + 128 : n2 + 256 * k + 256]
        else:
            b = jnp.zeros_like(a)
        x_new = jnp.where(low, pltpu.roll(a, p_size, 1), b)
        z_new = jnp.where(low, a, pltpu.roll(b, p_size, 1))
        xf = (x_new * r).astype(BF16)
        xf_buf[k] = xf
        xc = silu(pre_x[k] + xf.astype(F32) * par[0, k])
        sk = spread(step, k)
        dk = spread(decay, k)
        sx = sk * xc
        stx[k] = sx
        dec[k] = dk
        q = q_buf[:, 128 * k : 128 * k + 128]
        y_out = dk * q + sx * bd + par[2, k] * xc
        gated = y_out * silu(z_new * r)
        sq = sq + gated * gated
        inner[:, 128 * k : 128 * k + 128] = (gated * par[1, k]).astype(BF16)
    squares = jnp.sum(sq, axis=1, keepdims=True)
    hi = squares.astype(BF16).astype(F32)
    lo = squares - hi
    sq_tile = jnp.where(lane == 0, hi, jnp.where(lane == 1, lo, 0.0)).astype(BF16)

    def rs_copy(src_t, dest, yy, zz):
        return pltpu.make_async_remote_copy(
            src_ref=send_buf.at[yy, pl.ds(pl.multiple_of(zz * rows, rows), rows), :],
            dst_ref=rs_buf.at[src_t],
            send_sem=rs_send.at[dest],
            recv_sem=rs_recv.at[src_t],
            device_id=dev(sec, dest),
            device_id_type=MESH,
        )

    for yo in FAR:
        yy = (my_y + yo) % SIDE
        if yo == FAR[0]:
            for cp in loads[1 + heads : 1 + heads + SIDE]:
                cp.wait()
        part = jnp.dot(
            inner[:, 0 : heads * p_size], w_o[yy], preferred_element_type=F32
        )
        send_buf[yy, :, 0:chunk] = part.astype(BF16)
        send_buf[yy, :, chunk : chunk + 128] = sq_tile
        for zo in FAR:
            zz = (my_z + zo) % SIDE
            dest = zz * SIDE + yy
            if yo == 0 and zo == 0:
                pltpu.make_async_copy(
                    send_buf.at[yy, pl.ds(pl.multiple_of(zz * rows, rows), rows), :],
                    rs_buf.at[me],
                    rs_recv.at[me],
                ).start()
            else:
                rs_copy(me, dest, yy, zz).start()

    tot = jnp.zeros((rows, chunk + 128), F32)
    for yo in NEAR:
        for zo in NEAR:
            src = ((my_z + zo) % SIDE) * SIDE + (my_y + yo) % SIDE
            if yo == 0 and zo == 0:
                pltpu.make_async_copy(
                    send_buf.at[0, pl.ds(0, rows), :], rs_buf.at[src], rs_recv.at[src]
                ).wait()
            else:
                rs_copy(src, me, my_y, my_z).wait_recv()
            tot = tot + rs_buf[src].astype(F32)
    scale = lax.rsqrt(
        jnp.sum(tot[:, chunk : chunk + 128], axis=1, keepdims=True)
        * (1.0 / (heads * p_size * team))
        + epsilon
    )
    mine = hbuf[my_y, pl.ds(pl.multiple_of(my_z * rows, rows), rows), :].astype(F32)
    ag_src[...] = (mine + tot[:, 0:chunk] * scale).astype(BF16)

    @pl.when(sec < last)
    def _():
        for yo in FAR:
            for zo in FAR:
                ag_copy(me, ((my_z + zo) % SIDE) * SIDE + (my_y + yo) % SIDE).start()

    def sh_copy(src_z, j):
        return pltpu.make_async_remote_copy(
            src_ref=ag_src,
            dst_ref=sh_buf.at[src_z],
            send_sem=sh_send.at[j],
            recv_sem=sh_recv.at[src_z],
            device_id=dev(sec, my_y * SIDE + j),
            device_id_type=MESH,
        )

    def sh_own():
        return pltpu.make_async_copy(ag_src, sh_buf.at[my_z], sh_recv.at[my_z])

    for j in range(SIDE):
        own = my_y * SIDE + j == me

        @pl.when(own)
        def _():
            sh_own().start()

        @pl.when(jnp.logical_not(own))
        def _():
            sh_copy(my_z, j).start()

    zeros = jnp.zeros((128 - streams, 128), F32)
    for k in range(pairs):
        stx_t[128 * k : 128 * k + 128] = jnp.concatenate([stx[k], zeros], axis=0).T
        dec_t[128 * k : 128 * k + 128] = jnp.concatenate([dec[k], zeros], axis=0).T
    hp = heads * p_size
    octet = 8

    def out_copy(g):
        span = pl.ds(pl.multiple_of(g * octet, octet), octet)
        return pltpu.make_async_copy(st.at[span], ssm_out.at[span], out_sem.at[g])

    def update(g, carry):
        shift = (128 - g * octet) % 128
        b8 = b_buf[pl.ds(pl.multiple_of(g * octet, octet), octet), :]
        for half in range(heads):
            span = slice(p_size * half, p_size * half + p_size)
            sx_r = pltpu.roll(stx_t[span, :], shift, 1)
            dk_r = pltpu.roll(dec_t[span, :], shift, 1)
            for i in range(octet):
                old = st[g * octet + i, span, :].astype(F32)
                new = (
                    jnp.broadcast_to(dk_r[:, i : i + 1], (p_size, 128)) * old
                    + jnp.broadcast_to(sx_r[:, i : i + 1], (p_size, 128)) * b8[i : i + 1]
                )
                st[g * octet + i, span, :] = new.astype(BF16)
        out_copy(g).start()
        return carry

    lax.fori_loop(0, streams // octet, update, 0)

    cx_out[0] = cxs_ref[1]
    cx_out[1] = cxs_ref[2]
    for h in range(heads):
        xf = xf_buf[h // 2].astype(F32)
        cx_out[2, h] = xf[:, p_size * (h % 2) : p_size * (h % 2) + p_size].astype(BF16)

    for zz in range(SIDE):
        sh_copy(zz, 0).wait_recv()
    for yy in range(SIDE):

        @pl.when(my_y == yy)
        def _():
            for zz in range(SIDE):
                sec_out[rows * zz : rows * zz + rows, :] = (
                    sh_buf[zz].astype(F32)[:, share * yy : share * yy + share].astype(BF16)
                )

    for yo in FAR:
        for zo in FAR:
            dest = ((my_z + zo) % SIDE) * SIDE + (my_y + yo) % SIDE
            if not (yo == 0 and zo == 0):
                rs_copy(me, dest, my_y, my_z).wait_send()

    @pl.when(sec < last)
    def _():
        for dest in range(team):
            ag_copy(me, dest).wait_send()

    for j in range(SIDE):

        @pl.when(my_y * SIDE + j != me)
        def _():
            sh_copy(my_z, j).wait_send()

    @pl.when(sec == 0)
    def _():
        def sent(j, carry):
            init_copy((me + j) % team).wait_send()
            return carry

        lax.fori_loop(1, team, sent, 0)

    def written(g, carry):
        out_copy(g).wait()
        return carry

    lax.fori_loop(0, streams // octet, written, 0)


def shards(
    hidden_in,
    pre_gain,
    w_zx,
    w_bc,
    w_dt,
    dt_bias,
    a_log,
    d_skip,
    conv_x_weight,
    conv_x_bias,
    conv_bc_weight,
    conv_bc_bias,
    inner_gain,
    w_out,
    conv_x_state,
    conv_bc_state,
    ssm_state,
    sections,
):
    streams, share = hidden_in.shape
    _, heads, p_size, width = w_out.shape
    n2 = w_bc.shape[2]
    n_state = n2 // 2
    team = SIDE * SIDE
    chunk, rows = width // SIDE, streams // SIDE
    hp = heads * p_size
    cols = n2 + 128 * heads + 128
    pairs = (heads + 1) // 2
    args = (
        hidden_in,
        pre_gain,
        jnp.transpose(w_zx[0], (1, 0, 2)),
        w_bc[0],
        jnp.transpose(w_dt[0], (1, 0)),
        dt_bias,
        a_log,
        d_skip,
        jnp.transpose(conv_x_weight[0], (1, 0, 2)),
        jnp.transpose(conv_x_bias, (1, 0, 2)),
        conv_bc_weight[0],
        conv_bc_bias,
        jnp.transpose(inner_gain, (1, 0, 2)),
        w_out[0].reshape(hp, width),
        jnp.transpose(conv_x_state[0], (1, 2, 0, 3)),
        jnp.transpose(conv_bc_state[0], (1, 0, 2)),
        ssm_state[0].reshape(streams, hp, n_state),
    )
    vmem = pl.BlockSpec(memory_space=pltpu.VMEM)
    hbm = pl.BlockSpec(memory_space=pl.ANY)
    large = (2, 3, 13, 16)
    dma = pltpu.SemaphoreType.DMA
    sec_new, cx_new, cb_new, ssm_new = pl.pallas_call(
        functools.partial(kernel, sections),
        out_shape=(
            jax.ShapeDtypeStruct((streams, share), BF16),
            jax.ShapeDtypeStruct((3, heads, streams, p_size), BF16),
            jax.ShapeDtypeStruct((3, streams, n2), BF16),
            jax.ShapeDtypeStruct((streams, hp, n_state), BF16),
        ),
        in_specs=[hbm if i in large else vmem for i in range(len(args))],
        out_specs=(vmem, vmem, vmem, hbm),
        scratch_shapes=[
            pltpu.VMEM((width, cols), BF16),
            pltpu.VMEM((SIDE, hp, chunk), BF16),
            pltpu.VMEM((streams, hp, n_state), BF16),
            pltpu.VMEM((SIDE, streams, chunk), BF16),
            pltpu.VMEM((streams, cols), F32),
            pltpu.VMEM((128, width), F32),
            pltpu.VMEM((streams, n2), F32),
            pltpu.VMEM((pairs, streams, 128), F32),
            pltpu.VMEM((3, pairs, 1, 128), F32),
            pltpu.VMEM((streams, 128 * pairs), F32),
            pltpu.VMEM((streams, 128 * pairs), BF16),
            pltpu.VMEM((pairs, streams, 128), F32),
            pltpu.VMEM((pairs, streams, 128), F32),
            pltpu.VMEM((streams, n_state), F32),
            pltpu.VMEM((pairs, streams, 128), BF16),
            pltpu.VMEM((128 * pairs, 128), F32),
            pltpu.VMEM((128 * pairs, 128), F32),
            pltpu.VMEM((SIDE, streams, chunk + 128), BF16),
            pltpu.VMEM((team, rows, chunk + 128), BF16),
            pltpu.VMEM((rows, chunk), BF16),
            pltpu.VMEM((team, streams, share), BF16),
            pltpu.VMEM((SIDE, rows, chunk), BF16),
            dma((1 + heads + SIDE + 1,)),
            dma((8,)),
            dma((team,)),
            dma((team,)),
            dma((team,)),
            dma((team,)),
            dma((team,)),
            dma((team,)),
            dma((SIDE,)),
            dma((SIDE,)),
        ],
        compiler_params=pltpu.CompilerParams(
            collective_id=0, has_side_effects=True, vmem_limit_bytes=40 * 1024 * 1024
        ),
        name="stack_step",
    )(*args)
    return (
        sec_new[None],
        jnp.transpose(cx_new, (2, 0, 1, 3))[None],
        jnp.transpose(cb_new, (1, 0, 2))[None],
        ssm_new.reshape(ssm_state.shape),
    )


def solution(mesh):
    placed = (
        P(None, "tensor"),
        P("section", None),
        P("section", None, "tensor", None),
        P("section", None, None),
        P("section", None, "tensor"),
        P("section", "tensor"),
        P("section", "tensor"),
        P("section", "tensor"),
        P("section", None, "tensor", None),
        P("section", "tensor", None),
        P("section", None, None),
        P("section", None),
        P("section", "tensor", None),
        P("section", "tensor", None, None),
        P("section", None, None, "tensor", None),
        P("section", None, None, None),
        P("section", None, "tensor", None, None),
    )
    return jax.shard_map(
        functools.partial(shards, sections=mesh.shape["section"]),
        mesh=mesh,
        in_specs=placed,
        out_specs=(
            P("section", None, "tensor"),
            P("section", None, None, "tensor", None),
            P("section", None, None, None),
            P("section", None, "tensor", None, None),
        ),
        check_vma=False,
    )
```

```python
import functools

import jax
import jax.numpy as jnp
from jax import lax
from jax.experimental import pallas as pl
from jax.experimental.pallas import tpu as pltpu
from jax.sharding import PartitionSpec as P

epsilon = 1e-05
MESH = pl.DeviceIdType.MESH
F32, BF16 = jnp.float32, jnp.bfloat16
SIDE = 4
NEAR = (0, 1, 3, 2)
FAR = (2, 1, 3, 0)


def silu(v):
    return v / (1.0 + jnp.exp(-v))


def softplus(v):
    return jnp.maximum(v, 0.0) + jnp.log1p(jnp.exp(-jnp.abs(v)))


def kernel(
    sections,
    hid_ref,
    gain_hbm,
    wzx_hbm,
    wbc_hbm,
    wdt_hbm,
    dtb_hbm,
    alog_hbm,
    dsk_hbm,
    cxw_hbm,
    cxb_hbm,
    cbw_hbm,
    cbb_hbm,
    ig_hbm,
    wout_hbm,
    cxs_hbm,
    cbs_hbm,
    ssm_hbm,
    sec_out,
    cx_out,
    cb_out,
    st,
    gain_ref,
    wdt_ref,
    dtb_ref,
    alog_ref,
    dsk_ref,
    cxw_ref,
    cxb_ref,
    cbw_ref,
    cbb_ref,
    ig_ref,
    cxs_ref,
    cbs_ref,
    w_all,
    w_o,
    hbuf,
    acc,
    wdt_pad,
    pre_bc,
    pre_x,
    par,
    q_buf,
    inner,
    stx,
    dec,
    b_buf,
    xf_buf,
    stx_t,
    dec_t,
    send_buf,
    rs_buf,
    ag_src,
    init_buf,
    sh_buf,
    load_sem,
    small_sem,
    init_send,
    init_recv,
    rs_send,
    rs_recv,
    ag_send,
    ag_recv,
    sh_send,
    sh_recv,
):
    heads, streams, p_size = cxs_hbm.shape[1:]
    width, n2 = wbc_hbm.shape
    n_state = n2 // 2
    chunk = width // SIDE
    rows = streams // SIDE
    share = hid_ref.shape[1]
    team = SIDE * SIDE
    last = sections - 1

    sec = lax.axis_index("section")
    me = lax.axis_index("tensor")
    my_z = me // SIDE
    my_y = me % SIDE

    def dev(s, t):
        return {"section": s, "tensor": t}

    loads = [pltpu.make_async_copy(wbc_hbm, w_all.at[:, pl.ds(0, n2)], load_sem.at[0])]
    for h in range(heads):
        loads.append(
            pltpu.make_async_copy(
                wzx_hbm.at[h], w_all.at[:, pl.ds(n2 + 128 * h, 128)], load_sem.at[1 + h]
            )
        )
    at = 1 + heads
    for yy in range(SIDE):
        loads.append(
            pltpu.make_async_copy(
                wout_hbm.at[:, pl.ds(chunk * yy, chunk)], w_o.at[yy], load_sem.at[at + yy]
            )
        )
    at += SIDE
    loads.append(pltpu.make_async_copy(ssm_hbm, st, load_sem.at[at]))
    smalls = [
        pltpu.make_async_copy(a, b, small_sem.at[i])
        for i, (a, b) in enumerate(
            (
                (wdt_hbm, wdt_ref),
                (gain_hbm, gain_ref),
                (dtb_hbm, dtb_ref),
                (alog_hbm, alog_ref),
                (dsk_hbm, dsk_ref),
                (cxw_hbm, cxw_ref),
                (cxb_hbm, cxb_ref),
                (cbw_hbm, cbw_ref),
                (cbb_hbm, cbb_ref),
                (ig_hbm, ig_ref),
                (cxs_hbm, cxs_ref),
                (cbs_hbm, cbs_ref),
            )
        )
    ]

    barrier = pltpu.get_barrier_semaphore()

    def greet(j, carry):
        other = (me + j) % team

        @pl.when(j > 0)
        def _():
            pl.semaphore_signal(barrier, inc=1, device_id=dev(sec, other), device_id_type=MESH)

        @pl.when(sec > 0)
        def _():
            pl.semaphore_signal(barrier, inc=1, device_id=dev(sec - 1, other), device_id_type=MESH)

        @pl.when(sec < last)
        def _():
            pl.semaphore_signal(barrier, inc=1, device_id=dev(sec + 1, other), device_id_type=MESH)

        return carry

    for cp in smalls + loads:
        cp.start()
    lax.fori_loop(0, team, greet, 0)
    partners = team - 1 + jnp.where(sec > 0, team, 0) + jnp.where(sec < last, team, 0)
    pl.semaphore_wait(barrier, partners)

    def init_copy(dest):
        return pltpu.make_async_remote_copy(
            src_ref=hid_ref,
            dst_ref=init_buf.at[me],
            send_sem=init_send.at[dest],
            recv_sem=init_recv.at[me],
            device_id=dev(sec, dest),
            device_id_type=MESH,
        )

    def init_own():
        return pltpu.make_async_copy(hid_ref, init_buf.at[me], init_recv.at[me])

    @pl.when(sec == 0)
    def _():
        def go(j, carry):
            init_copy((me + j) % team).start()
            return carry

        lax.fori_loop(1, team, go, 0)
        init_own().start()

    lane = lax.broadcasted_iota(jnp.int32, (streams, 128), 1)
    low = lane < p_size
    for cp in smalls:
        cp.wait()
    wdt_pad[...] = jnp.zeros_like(wdt_pad)
    wdt_pad[0:heads, :] = wdt_ref[...].astype(F32)
    for h in range(1 + heads):
        loads[h].wait()
    for j in range(width // 128):
        blk = wdt_pad[:, 128 * j : 128 * j + 128]
        w_all[128 * j : 128 * j + 128, n2 + 128 * heads : n2 + 128 * heads + 128] = blk.T.astype(BF16)
    acc[...] = jnp.zeros_like(acc)
    q_buf[...] = jnp.zeros_like(q_buf)
    cbw = cbw_ref[...]
    pre_bc[...] = (
        cbs_ref[0].astype(F32) * cbw[0:1]
        + cbs_ref[1].astype(F32) * cbw[1:2]
        + cbs_ref[2].astype(F32) * cbw[2:3]
        + cbb_ref[...]
    )
    pairs = (heads + 1) // 2

    def packed(get, k):
        a = get(2 * k)
        b = get(2 * k + 1) if 2 * k + 1 < heads else jnp.zeros_like(a)
        return jnp.concatenate([a, b], axis=1)

    def pre_of(h):
        w = cxw_ref[h]
        return (
            cxs_ref[0, h].astype(F32) * w[0:1]
            + cxs_ref[1, h].astype(F32) * w[1:2]
            + cxs_ref[2, h].astype(F32) * w[2:3]
            + cxb_ref[h]
        )

    for k in range(pairs):
        pre_x[k] = packed(pre_of, k)
        par[0, k] = packed(lambda h: cxw_ref[h][3:4], k)
        par[1, k] = packed(lambda h: ig_ref[h], k)
        par[2, k] = packed(
            lambda h: jnp.broadcast_to(dsk_ref[:, h : h + 1], (1, p_size)), k
        )
    pad = jnp.zeros((1, 128 - heads), F32)
    dtb = jnp.concatenate([dtb_ref[...], pad], axis=1)
    neg_a = -jnp.exp(jnp.concatenate([alog_ref[...], pad], axis=1))

    @pl.when(sec == 0)
    def _():
        def wait_one(k, carry):
            pltpu.make_async_copy(hid_ref, init_buf.at[k], init_recv.at[k]).wait()
            return carry

        lax.fori_loop(0, team, wait_one, 0)
        for yy in range(SIDE):
            parts = [init_buf[SIDE * yy + i].astype(F32) for i in range(SIDE)]
            hbuf[yy] = jnp.concatenate(parts, axis=1).astype(BF16)

    def ag_copy(src_t, dest):
        return pltpu.make_async_remote_copy(
            src_ref=ag_src,
            dst_ref=hbuf.at[src_t % SIDE, pl.ds(pl.multiple_of((src_t // SIDE) * rows, rows), rows), :],
            send_sem=ag_send.at[dest],
            recv_sem=ag_recv.at[src_t],
            device_id=dev(jnp.minimum(sec + 1, last), dest),
            device_id_type=MESH,
        )

    sq = jnp.zeros((streams, 128), F32)
    for off in NEAR:
        yy = (my_y + off) % SIDE

        @pl.when(sec > 0)
        def _():
            for zo in NEAR:
                ag_copy(((my_z + zo) % SIDE) * SIDE + yy, me).wait_recv()

        hv = hbuf[yy].astype(F32)
        for i in range(chunk // 128):
            part = hv[:, 128 * i : 128 * i + 128]
            sq = sq + part * part
        start = pl.multiple_of(yy * chunk, chunk)
        hg = (hv * gain_ref[:, pl.ds(start, chunk)]).astype(BF16)
        acc[...] += jnp.dot(hg, w_all[pl.ds(start, chunk), :], preferred_element_type=F32)
    r = lax.rsqrt(jnp.sum(sq, axis=1, keepdims=True) * (1.0 / width) + epsilon)

    bcf = (acc[:, 0:n2] * r).astype(BF16)
    cb_out[0] = cbs_ref[1]
    cb_out[1] = cbs_ref[2]
    cb_out[2] = bcf
    bcv = silu(pre_bc[...] + bcf.astype(F32) * cbw[3:4])
    b_in = bcv[:, 0:n_state]
    c_out = bcv[:, n_state:n2]
    b_buf[...] = b_in
    bd = jnp.sum(b_in * c_out, axis=1, keepdims=True)
    c_bf = c_out

    loads[-1].wait()
    group = 16
    row = lax.broadcasted_iota(jnp.int32, (group, n_state), 0)
    for g in range(streams // group):
        c16 = c_bf[group * g : group * g + group]
        total = None
        for i in range(0, group, 2):
            lhs = jnp.concatenate(
                [jnp.where(row == i, c16, 0.0), jnp.where(row == i + 1, c16, 0.0)], axis=1
            ).astype(BF16)
            rhs = jnp.concatenate([st[group * g + i], st[group * g + i + 1]], axis=1)
            term = lax.dot_general(
                lhs, rhs, (((1,), (1,)), ((), ())), preferred_element_type=F32
            )
            total = term if total is None else total + term
        q_buf[group * g : group * g + group, 0 : heads * p_size] = total

    dt0 = n2 + 128 * heads
    step = softplus(acc[:, dt0 : dt0 + 128] * r + dtb)
    decay = jnp.exp(step * neg_a)

    def spread(v, k):
        hi = min(2 * k + 1, heads - 1)
        a = jnp.broadcast_to(v[:, 2 * k : 2 * k + 1], (streams, 128))
        b = jnp.broadcast_to(v[:, hi : hi + 1], (streams, 128))
        return jnp.where(low, a, b)

    sq = jnp.zeros((streams, 128), F32)
    for k in range(pairs):
        a = acc[:, n2 + 256 * k : n2 + 256 * k + 128]
        if 2 * k + 1 < heads:
            b = acc[:, n2 + 256 * k + 128 : n2 + 256 * k + 256]
        else:
            b = jnp.zeros_like(a)
        x_new = jnp.where(low, pltpu.roll(a, p_size, 1), b)
        z_new = jnp.where(low, a, pltpu.roll(b, p_size, 1))
        xf = (x_new * r).astype(BF16)
        xf_buf[k] = xf
        xc = silu(pre_x[k] + xf.astype(F32) * par[0, k])
        sk = spread(step, k)
        dk = spread(decay, k)
        sx = sk * xc
        stx[k] = sx
        dec[k] = dk
        q = q_buf[:, 128 * k : 128 * k + 128]
        y_out = dk * q + sx * bd + par[2, k] * xc
        gated = y_out * silu(z_new * r)
        sq = sq + gated * gated
        inner[:, 128 * k : 128 * k + 128] = (gated * par[1, k]).astype(BF16)
    squares = jnp.sum(sq, axis=1, keepdims=True)
    hi = squares.astype(BF16).astype(F32)
    lo = squares - hi
    sq_tile = jnp.where(lane == 0, hi, jnp.where(lane == 1, lo, 0.0)).astype(BF16)

    def rs_copy(src_t, dest, yy, zz):
        return pltpu.make_async_remote_copy(
            src_ref=send_buf.at[yy, pl.ds(pl.multiple_of(zz * rows, rows), rows), :],
            dst_ref=rs_buf.at[src_t],
            send_sem=rs_send.at[dest],
            recv_sem=rs_recv.at[src_t],
            device_id=dev(sec, dest),
            device_id_type=MESH,
        )

    for yo in FAR:
        yy = (my_y + yo) % SIDE
        if yo == FAR[0]:
            for cp in loads[1 + heads : 1 + heads + SIDE]:
                cp.wait()
        part = jnp.dot(
            inner[:, 0 : heads * p_size], w_o[yy], preferred_element_type=F32
        )
        send_buf[yy, :, 0:chunk] = part.astype(BF16)
        send_buf[yy, :, chunk : chunk + 128] = sq_tile
        for zo in FAR:
            zz = (my_z + zo) % SIDE
            dest = zz * SIDE + yy
            if yo == 0 and zo == 0:
                pltpu.make_async_copy(
                    send_buf.at[yy, pl.ds(pl.multiple_of(zz * rows, rows), rows), :],
                    rs_buf.at[me],
                    rs_recv.at[me],
                ).start()
            else:
                rs_copy(me, dest, yy, zz).start()

    tot = jnp.zeros((rows, chunk + 128), F32)
    for yo in NEAR:
        for zo in NEAR:
            src = ((my_z + zo) % SIDE) * SIDE + (my_y + yo) % SIDE
            if yo == 0 and zo == 0:
                pltpu.make_async_copy(
                    send_buf.at[0, pl.ds(0, rows), :], rs_buf.at[src], rs_recv.at[src]
                ).wait()
            else:
                rs_copy(src, me, my_y, my_z).wait_recv()
            tot = tot + rs_buf[src].astype(F32)
    scale = lax.rsqrt(
        jnp.sum(tot[:, chunk : chunk + 128], axis=1, keepdims=True)
        * (1.0 / (heads * p_size * team))
        + epsilon
    )
    mine = hbuf[my_y, pl.ds(pl.multiple_of(my_z * rows, rows), rows), :].astype(F32)
    ag_src[...] = (mine + tot[:, 0:chunk] * scale).astype(BF16)

    @pl.when(sec < last)
    def _():
        for yo in FAR:
            for zo in FAR:
                ag_copy(me, ((my_z + zo) % SIDE) * SIDE + (my_y + yo) % SIDE).start()

    def sh_copy(src_z, j):
        return pltpu.make_async_remote_copy(
            src_ref=ag_src,
            dst_ref=sh_buf.at[src_z],
            send_sem=sh_send.at[j],
            recv_sem=sh_recv.at[src_z],
            device_id=dev(sec, my_y * SIDE + j),
            device_id_type=MESH,
        )

    def sh_own():
        return pltpu.make_async_copy(ag_src, sh_buf.at[my_z], sh_recv.at[my_z])

    for j in range(SIDE):
        own = my_y * SIDE + j == me

        @pl.when(own)
        def _():
            sh_own().start()

        @pl.when(jnp.logical_not(own))
        def _():
            sh_copy(my_z, j).start()

    zeros = jnp.zeros((128 - streams, 128), F32)
    for k in range(pairs):
        stx_t[128 * k : 128 * k + 128] = jnp.concatenate([stx[k], zeros], axis=0).T
        dec_t[128 * k : 128 * k + 128] = jnp.concatenate([dec[k], zeros], axis=0).T
    hp = heads * p_size
    octet = 8

    def update(g, carry):
        shift = (128 - g * octet) % 128
        b8 = b_buf[pl.ds(pl.multiple_of(g * octet, octet), octet), :]
        for half in range(heads):
            span = slice(p_size * half, p_size * half + p_size)
            sx_r = pltpu.roll(stx_t[span, :], shift, 1)
            dk_r = pltpu.roll(dec_t[span, :], shift, 1)
            for i in range(octet):
                old = st[g * octet + i, span, :].astype(F32)
                new = (
                    jnp.broadcast_to(dk_r[:, i : i + 1], (p_size, 128)) * old
                    + jnp.broadcast_to(sx_r[:, i : i + 1], (p_size, 128)) * b8[i : i + 1]
                )
                st[g * octet + i, span, :] = new.astype(BF16)
        return carry

    lax.fori_loop(0, streams // octet, update, 0)

    cx_out[0] = cxs_ref[1]
    cx_out[1] = cxs_ref[2]
    for h in range(heads):
        xf = xf_buf[h // 2].astype(F32)
        cx_out[2, h] = xf[:, p_size * (h % 2) : p_size * (h % 2) + p_size].astype(BF16)

    for zz in range(SIDE):
        sh_copy(zz, 0).wait_recv()
    for yy in range(SIDE):

        @pl.when(my_y == yy)
        def _():
            for zz in range(SIDE):
                sec_out[rows * zz : rows * zz + rows, :] = (
                    sh_buf[zz].astype(F32)[:, share * yy : share * yy + share].astype(BF16)
                )

    for yo in FAR:
        for zo in FAR:
            dest = ((my_z + zo) % SIDE) * SIDE + (my_y + yo) % SIDE
            if not (yo == 0 and zo == 0):
                rs_copy(me, dest, my_y, my_z).wait_send()

    @pl.when(sec < last)
    def _():
        for dest in range(team):
            ag_copy(me, dest).wait_send()

    for j in range(SIDE):

        @pl.when(my_y * SIDE + j != me)
        def _():
            sh_copy(my_z, j).wait_send()

    @pl.when(sec == 0)
    def _():
        def sent(j, carry):
            init_copy((me + j) % team).wait_send()
            return carry

        lax.fori_loop(1, team, sent, 0)


def shards(
    hidden_in,
    pre_gain,
    w_zx,
    w_bc,
    w_dt,
    dt_bias,
    a_log,
    d_skip,
    conv_x_weight,
    conv_x_bias,
    conv_bc_weight,
    conv_bc_bias,
    inner_gain,
    w_out,
    conv_x_state,
    conv_bc_state,
    ssm_state,
    sections,
):
    streams, share = hidden_in.shape
    _, heads, p_size, width = w_out.shape
    n2 = w_bc.shape[2]
    n_state = n2 // 2
    team = SIDE * SIDE
    chunk, rows = width // SIDE, streams // SIDE
    hp = heads * p_size
    cols = n2 + 128 * heads + 128
    pairs = (heads + 1) // 2
    args = (
        hidden_in,
        pre_gain,
        jnp.transpose(w_zx[0], (1, 0, 2)),
        w_bc[0],
        jnp.transpose(w_dt[0], (1, 0)),
        dt_bias,
        a_log,
        d_skip,
        jnp.transpose(conv_x_weight[0], (1, 0, 2)),
        jnp.transpose(conv_x_bias, (1, 0, 2)),
        conv_bc_weight[0],
        conv_bc_bias,
        jnp.transpose(inner_gain, (1, 0, 2)),
        w_out[0].reshape(hp, width),
        jnp.transpose(conv_x_state[0], (1, 2, 0, 3)),
        jnp.transpose(conv_bc_state[0], (1, 0, 2)),
        ssm_state[0].reshape(streams, hp, n_state),
    )
    vmem = pl.BlockSpec(memory_space=pltpu.VMEM)
    hbm = pl.BlockSpec(memory_space=pltpu.HBM)
    small = (1, 4, 5, 6, 7, 8, 9, 10, 11, 12, 14, 15)
    dma = pltpu.SemaphoreType.DMA
    sec_new, cx_new, cb_new, ssm_new = pl.pallas_call(
        functools.partial(kernel, sections),
        out_shape=(
            jax.ShapeDtypeStruct((streams, share), BF16),
            jax.ShapeDtypeStruct((3, heads, streams, p_size), BF16),
            jax.ShapeDtypeStruct((3, streams, n2), BF16),
            jax.ShapeDtypeStruct((streams, hp, n_state), BF16),
        ),
        in_specs=[hbm] * len(args),
        out_specs=(vmem, vmem, vmem, vmem),
        scratch_shapes=[pltpu.VMEM(args[i].shape, args[i].dtype) for i in small]
        + [
            pltpu.VMEM((width, cols), BF16),
            pltpu.VMEM((SIDE, hp, chunk), BF16),
            pltpu.VMEM((SIDE, streams, chunk), BF16),
            pltpu.VMEM((streams, cols), F32),
            pltpu.VMEM((128, width), F32),
            pltpu.VMEM((streams, n2), F32),
            pltpu.VMEM((pairs, streams, 128), F32),
            pltpu.VMEM((3, pairs, 1, 128), F32),
            pltpu.VMEM((streams, 128 * pairs), F32),
            pltpu.VMEM((streams, 128 * pairs), BF16),
            pltpu.VMEM((pairs, streams, 128), F32),
            pltpu.VMEM((pairs, streams, 128), F32),
            pltpu.VMEM((streams, n_state), F32),
            pltpu.VMEM((pairs, streams, 128), BF16),
            pltpu.VMEM((128 * pairs, 128), F32),
            pltpu.VMEM((128 * pairs, 128), F32),
            pltpu.VMEM((SIDE, streams, chunk + 128), BF16),
            pltpu.VMEM((team, rows, chunk + 128), BF16),
            pltpu.VMEM((rows, chunk), BF16),
            pltpu.VMEM((team, streams, share), BF16),
            pltpu.VMEM((SIDE, rows, chunk), BF16),
            dma((1 + heads + SIDE + 1,)),
            dma((len(small),)),
            dma((team,)),
            dma((team,)),
            dma((team,)),
            dma((team,)),
            dma((team,)),
            dma((team,)),
            dma((SIDE,)),
            dma((SIDE,)),
        ],
        compiler_params=pltpu.CompilerParams(
            collective_id=0, has_side_effects=True, vmem_limit_bytes=40 * 1024 * 1024
        ),
        name="stack_step",
    )(*[pltpu.with_memory_space_constraint(a, pltpu.HBM) for a in args])
    return (
        sec_new[None],
        jnp.transpose(cx_new, (2, 0, 1, 3))[None],
        jnp.transpose(cb_new, (1, 0, 2))[None],
        ssm_new.reshape(ssm_state.shape),
    )


def solution(mesh):
    placed = (
        P(None, "tensor"),
        P("section", None),
        P("section", None, "tensor", None),
        P("section", None, None),
        P("section", None, "tensor"),
        P("section", "tensor"),
        P("section", "tensor"),
        P("section", "tensor"),
        P("section", None, "tensor", None),
        P("section", "tensor", None),
        P("section", None, None),
        P("section", None),
        P("section", "tensor", None),
        P("section", "tensor", None, None),
        P("section", None, None, "tensor", None),
        P("section", None, None, None),
        P("section", None, "tensor", None, None),
    )
    return jax.shard_map(
        functools.partial(shards, sections=mesh.shape["section"]),
        mesh=mesh,
        in_specs=placed,
        out_specs=(
            P("section", None, "tensor"),
            P("section", None, None, "tensor", None),
            P("section", None, None, None),
            P("section", None, "tensor", None, None),
        ),
        check_vma=False,
    )
```

```python
import functools

import jax
import jax.numpy as jnp
from jax import lax
from jax.experimental import pallas as pl
from jax.experimental.pallas import tpu as pltpu
from jax.sharding import PartitionSpec as P

epsilon = 1e-05
MESH = pl.DeviceIdType.MESH
F32, BF16 = jnp.float32, jnp.bfloat16
SIDE = 4
NEAR = (0, 1, 3, 2)
FAR = (2, 1, 3, 0)
BLOCKS = 2
EARLY = (1, 3)


def silu(v):
    return v / (1.0 + jnp.exp(-v))


def softplus(v):
    return jnp.maximum(v, 0.0) + jnp.log1p(jnp.exp(-jnp.abs(v)))


def kernel(
    sections,
    hid_ref,
    gain_hbm,
    wzx_hbm,
    wbc_hbm,
    wdt_hbm,
    dtb_hbm,
    alog_hbm,
    dsk_hbm,
    cxw_hbm,
    cxb_hbm,
    cbw_hbm,
    cbb_hbm,
    ig_hbm,
    wout_hbm,
    cxs_hbm,
    cbs_hbm,
    ssm_hbm,
    sec_out,
    cx_out,
    cb_out,
    st,
    gain_ref,
    wdt_ref,
    dtb_ref,
    alog_ref,
    dsk_ref,
    cxw_ref,
    cxb_ref,
    cbw_ref,
    cbb_ref,
    ig_ref,
    cxs_ref,
    cbs_ref,
    w_all,
    w_o,
    hbuf,
    acc,
    wdt_pad,
    pre_bc,
    pre_x,
    par,
    q_buf,
    inner,
    stx,
    dec,
    b_buf,
    xf_buf,
    stx_t,
    send_buf,
    rs_buf,
    ag_src,
    init_buf,
    sh_buf,
    load_sem,
    small_sem,
    init_send,
    init_recv,
    rs_send,
    rs_recv,
    ag_send,
    ag_recv,
    sh_send,
    sh_recv,
):
    heads, streams, p_size = cxs_hbm.shape[1:]
    width, n2 = wbc_hbm.shape
    n_state = n2 // 2
    chunk = width // SIDE
    block = streams // BLOCKS
    rows = block // SIDE
    share = hid_ref.shape[1]
    team = SIDE * SIDE
    last = sections - 1

    sec = lax.axis_index("section")
    me = lax.axis_index("tensor")
    my_z = me // SIDE
    my_y = me % SIDE

    def dev(s, t):
        return {"section": s, "tensor": t}

    loads = [pltpu.make_async_copy(wbc_hbm, w_all.at[:, pl.ds(0, n2)], load_sem.at[0])]
    for h in range(heads):
        loads.append(
            pltpu.make_async_copy(
                wzx_hbm.at[h], w_all.at[:, pl.ds(n2 + 128 * h, 128)], load_sem.at[1 + h]
            )
        )
    at = 1 + heads
    for yy in range(SIDE):
        loads.append(
            pltpu.make_async_copy(
                wout_hbm.at[:, pl.ds(chunk * yy, chunk)], w_o.at[yy], load_sem.at[at + yy]
            )
        )
    at += SIDE
    loads.append(pltpu.make_async_copy(ssm_hbm, st, load_sem.at[at]))
    smalls = [
        pltpu.make_async_copy(a, b, small_sem.at[i])
        for i, (a, b) in enumerate(
            (
                (wdt_hbm, wdt_ref),
                (gain_hbm, gain_ref),
                (dtb_hbm, dtb_ref),
                (alog_hbm, alog_ref),
                (dsk_hbm, dsk_ref),
                (cxw_hbm, cxw_ref),
                (cxb_hbm, cxb_ref),
                (cbw_hbm, cbw_ref),
                (cbb_hbm, cbb_ref),
                (ig_hbm, ig_ref),
                (cxs_hbm, cxs_ref),
                (cbs_hbm, cbs_ref),
            )
        )
    ]

    barrier = pltpu.get_barrier_semaphore()

    def greet(j, carry):
        other = (me + j) % team

        @pl.when(j > 0)
        def _():
            pl.semaphore_signal(barrier, inc=1, device_id=dev(sec, other), device_id_type=MESH)

        @pl.when(sec > 0)
        def _():
            pl.semaphore_signal(barrier, inc=1, device_id=dev(sec - 1, other), device_id_type=MESH)

        @pl.when(sec < last)
        def _():
            pl.semaphore_signal(barrier, inc=1, device_id=dev(sec + 1, other), device_id_type=MESH)

        return carry

    for cp in smalls + loads:
        cp.start()
    lax.fori_loop(0, team, greet, 0)
    partners = team - 1 + jnp.where(sec > 0, team, 0) + jnp.where(sec < last, team, 0)
    pl.semaphore_wait(barrier, partners)

    def init_copy(dest):
        return pltpu.make_async_remote_copy(
            src_ref=hid_ref,
            dst_ref=init_buf.at[me],
            send_sem=init_send.at[dest],
            recv_sem=init_recv.at[me],
            device_id=dev(sec, dest),
            device_id_type=MESH,
        )

    def init_own():
        return pltpu.make_async_copy(hid_ref, init_buf.at[me], init_recv.at[me])

    @pl.when(sec == 0)
    def _():
        def go(j, carry):
            init_copy((me + j) % team).start()
            return carry

        lax.fori_loop(1, team, go, 0)
        init_own().start()

    for cp in smalls:
        cp.wait()
    wdt_pad[...] = jnp.zeros_like(wdt_pad)
    wdt_pad[0:heads, :] = wdt_ref[...].astype(F32)
    for h in range(1 + heads):
        loads[h].wait()
    for j in range(width // 128):
        blk = wdt_pad[:, 128 * j : 128 * j + 128]
        w_all[128 * j : 128 * j + 128, n2 + 128 * heads : n2 + 128 * heads + 128] = blk.T.astype(BF16)
    q_buf[...] = jnp.zeros_like(q_buf)
    cb_out[0] = cbs_ref[1]
    cb_out[1] = cbs_ref[2]
    cx_out[0] = cxs_ref[1]
    cx_out[1] = cxs_ref[2]
    cbw = cbw_ref[...]
    pre_bc[...] = (
        cbs_ref[0].astype(F32) * cbw[0:1]
        + cbs_ref[1].astype(F32) * cbw[1:2]
        + cbs_ref[2].astype(F32) * cbw[2:3]
        + cbb_ref[...]
    )
    pairs = (heads + 1) // 2

    def packed(get, k):
        a = get(2 * k)
        b = get(2 * k + 1) if 2 * k + 1 < heads else jnp.zeros_like(a)
        return jnp.concatenate([a, b], axis=1)

    def pre_of(h):
        w = cxw_ref[h]
        return (
            cxs_ref[0, h].astype(F32) * w[0:1]
            + cxs_ref[1, h].astype(F32) * w[1:2]
            + cxs_ref[2, h].astype(F32) * w[2:3]
            + cxb_ref[h]
        )

    for k in range(pairs):
        pre_x[k] = packed(pre_of, k)
        par[0, k] = packed(lambda h: cxw_ref[h][3:4], k)
        par[1, k] = packed(lambda h: ig_ref[h], k)
        par[2, k] = packed(
            lambda h: jnp.broadcast_to(dsk_ref[:, h : h + 1], (1, p_size)), k
        )
    pad = jnp.zeros((1, 128 - heads), F32)
    dtb = jnp.concatenate([dtb_ref[...], pad], axis=1)
    neg_a = -jnp.exp(jnp.concatenate([alog_ref[...], pad], axis=1))

    @pl.when(sec == 0)
    def _():
        def wait_one(k, carry):
            pltpu.make_async_copy(hid_ref, init_buf.at[k], init_recv.at[k]).wait()
            return carry

        lax.fori_loop(0, team, wait_one, 0)
        for yy in range(SIDE):
            parts = [init_buf[SIDE * yy + i].astype(F32) for i in range(SIDE)]
            whole = jnp.concatenate(parts, axis=1)
            for blk in range(BLOCKS):
                for zz in range(SIDE):
                    at_row = blk * block + zz * rows
                    hbuf[blk, yy, zz] = whole[at_row : at_row + rows].astype(BF16)

    def ag_copy(blk, src_t, dest):
        return pltpu.make_async_remote_copy(
            src_ref=ag_src.at[blk],
            dst_ref=hbuf.at[blk, src_t % SIDE, src_t // SIDE],
            send_sem=ag_send.at[blk, dest],
            recv_sem=ag_recv.at[blk, src_t],
            device_id=dev(jnp.minimum(sec + 1, last), dest),
            device_id_type=MESH,
        )

    def rs_copy(blk, src_t, dest, yy, zz):
        return pltpu.make_async_remote_copy(
            src_ref=send_buf.at[blk, yy, zz],
            dst_ref=rs_buf.at[blk, src_t],
            send_sem=rs_send.at[blk, dest],
            recv_sem=rs_recv.at[blk, src_t],
            device_id=dev(sec, dest),
            device_id_type=MESH,
        )

    def rs_own(blk):
        return pltpu.make_async_copy(
            send_buf.at[blk, my_y, my_z], rs_buf.at[blk, me], rs_recv.at[blk, me]
        )

    for cp in loads[1 + heads :]:
        cp.wait()
    lane = lax.broadcasted_iota(jnp.int32, (block, 128), 1)
    low = lane < p_size
    hp = heads * p_size
    dt0 = n2 + 128 * heads
    group = 16
    row = lax.broadcasted_iota(jnp.int32, (group, n_state), 0)

    def layer(blk, carry):
        here = pl.ds(pl.multiple_of(blk * block, block), block)

        sq = jnp.zeros((block, 128), F32)
        for off in NEAR:
            yy = (my_y + off) % SIDE

            @pl.when(sec > 0)
            def _():
                for zo in NEAR:
                    ag_copy(blk, ((my_z + zo) % SIDE) * SIDE + yy, me).wait_recv()

            hv = jnp.concatenate([hbuf[blk, yy, zz].astype(F32) for zz in range(SIDE)], axis=0)
            for i in range(chunk // 128):
                part = hv[:, 128 * i : 128 * i + 128]
                sq = sq + part * part
            start = pl.multiple_of(yy * chunk, chunk)
            hg = (hv * gain_ref[:, pl.ds(start, chunk)]).astype(BF16)
            term = jnp.dot(hg, w_all[pl.ds(start, chunk), :], preferred_element_type=F32)
            if off == NEAR[0]:
                acc[...] = term
            else:
                acc[...] += term
        r = lax.rsqrt(jnp.sum(sq, axis=1, keepdims=True) * (1.0 / width) + epsilon)

        bcf = (acc[:, 0:n2] * r).astype(BF16)
        cb_out[2, here, :] = bcf
        bcv = silu(pre_bc[here, :] + bcf.astype(F32) * cbw_ref[3:4, :])
        b_in = bcv[:, 0:n_state]
        c_out = bcv[:, n_state:n2]
        b_buf[here, :] = b_in
        bd = jnp.sum(b_in * c_out, axis=1, keepdims=True)

        for g in range(block // group):
            c16 = c_out[group * g : group * g + group]
            base = blk * block + group * g
            total = None
            for i in range(0, group, 2):
                lhs = jnp.concatenate(
                    [jnp.where(row == i, c16, 0.0), jnp.where(row == i + 1, c16, 0.0)], axis=1
                ).astype(BF16)
                rhs = jnp.concatenate([st[base + i], st[base + i + 1]], axis=1)
                term = lax.dot_general(
                    lhs, rhs, (((1,), (1,)), ((), ())), preferred_element_type=F32
                )
                total = term if total is None else total + term
            q_buf[group * g : group * g + group, 0:hp] = total

        step = softplus(acc[:, dt0 : dt0 + 128] * r + dtb)
        decay = jnp.exp(step * neg_a)

        def each(v):
            return [jnp.broadcast_to(v[:, h : h + 1], (block, 128)) for h in range(heads)]

        steps, decays = each(step), each(decay)
        for h in range(heads):
            dec[h, here, :] = decays[h]

        def spread(v, k):
            return jnp.where(low, v[2 * k], v[min(2 * k + 1, heads - 1)])

        sq = jnp.zeros((block, 128), F32)
        for k in range(pairs):
            a = acc[:, n2 + 256 * k : n2 + 256 * k + 128]
            if 2 * k + 1 < heads:
                b = acc[:, n2 + 256 * k + 128 : n2 + 256 * k + 256]
            else:
                b = jnp.zeros_like(a)
            x_new = jnp.where(low, pltpu.roll(a, p_size, 1), b)
            z_new = jnp.where(low, a, pltpu.roll(b, p_size, 1))
            xf = (x_new * r).astype(BF16)
            xf_buf[k, here, :] = xf
            xc = silu(pre_x[k, here, :] + xf.astype(F32) * par[0, k])
            sx = spread(steps, k) * xc
            stx[k, here, :] = sx
            q = q_buf[:, 128 * k : 128 * k + 128]
            y_out = spread(decays, k) * q + sx * bd + par[2, k] * xc
            gated = y_out * silu(z_new * r)
            sq = sq + gated * gated
            inner[:, 128 * k : 128 * k + 128] = (gated * par[1, k]).astype(BF16)
        squares = jnp.sum(sq, axis=1, keepdims=True)
        hi = squares.astype(BF16).astype(F32)
        lo = squares - hi
        sq_tile = jnp.where(lane == 0, hi, jnp.where(lane == 1, lo, 0.0))

        for yo in FAR:
            yy = (my_y + yo) % SIDE
            part = jnp.dot(inner[:, 0:hp], w_o[yy], preferred_element_type=F32)
            whole = jnp.concatenate([part, sq_tile], axis=1)
            for zz in range(SIDE):
                send_buf[blk, yy, zz] = whole[rows * zz : rows * zz + rows].astype(BF16)
            for zo in FAR:
                zz = (my_z + zo) % SIDE
                if yo == 0 and zo == 0:
                    rs_own(blk).start()
                else:
                    rs_copy(blk, me, zz * SIDE + yy, yy, zz).start()
        return carry

    lax.fori_loop(0, BLOCKS, layer, 0)

    octet = 8
    per_block = block // octet

    def turn():
        zeros = jnp.zeros((128 - streams, 128), F32)
        for k in range(pairs):
            stx_t[128 * k : 128 * k + 128] = jnp.concatenate([stx[k], zeros], axis=0).T

    def update(g, carry):
        shift = (128 - g * octet) % 128
        span8 = pl.ds(pl.multiple_of(g * octet, octet), octet)
        b8 = b_buf[span8, :]
        for h in range(heads):
            span = slice(p_size * h, p_size * h + p_size)
            sx_r = pltpu.roll(stx_t[span, :], shift, 1)
            d8 = dec[h, span8, :]
            for i in range(octet):
                old = st[g * octet + i, span, :].astype(F32)
                new = d8[i : i + 1] * old + jnp.broadcast_to(
                    sx_r[:, i : i + 1], (p_size, 128)
                ) * b8[i : i + 1]
                st[g * octet + i, span, :] = new.astype(BF16)
        return carry

    def sh_copy(blk, src_z, j):
        return pltpu.make_async_remote_copy(
            src_ref=ag_src.at[blk],
            dst_ref=sh_buf.at[blk, src_z],
            send_sem=sh_send.at[blk, j],
            recv_sem=sh_recv.at[blk, src_z],
            device_id=dev(sec, my_y * SIDE + j),
            device_id_type=MESH,
        )

    turn()
    for blk in range(BLOCKS):
        lax.fori_loop(EARLY[blk - 1] if blk else 0, EARLY[blk], update, 0)

        tot = jnp.zeros((rows, chunk + 128), F32)
        for yo in NEAR:
            for zo in NEAR:
                src = ((my_z + zo) % SIDE) * SIDE + (my_y + yo) % SIDE
                if yo == 0 and zo == 0:
                    rs_own(blk).wait()
                else:
                    rs_copy(blk, src, me, my_y, my_z).wait_recv()
                tot = tot + rs_buf[blk, src].astype(F32)
        scale = lax.rsqrt(
            jnp.sum(tot[:, chunk : chunk + 128], axis=1, keepdims=True) * (1.0 / (hp * team))
            + epsilon
        )
        mine = hbuf[blk, my_y, my_z].astype(F32)
        ag_src[blk] = (mine + tot[:, 0:chunk] * scale).astype(BF16)

        @pl.when(sec < last)
        def _():
            for yo in FAR:
                for zo in FAR:
                    ag_copy(blk, me, ((my_z + zo) % SIDE) * SIDE + (my_y + yo) % SIDE).start()

        for j in range(SIDE):
            own = my_y * SIDE + j == me

            @pl.when(own)
            def _():
                pltpu.make_async_copy(
                    ag_src.at[blk], sh_buf.at[blk, my_z], sh_recv.at[blk, my_z]
                ).start()

            @pl.when(jnp.logical_not(own))
            def _():
                sh_copy(blk, my_z, j).start()

    lax.fori_loop(EARLY[-1], streams // octet, update, 0)

    for h in range(heads):
        xf = xf_buf[h // 2].astype(F32)
        cx_out[2, h] = xf[:, p_size * (h % 2) : p_size * (h % 2) + p_size].astype(BF16)

    for blk in range(BLOCKS):
        for zz in range(SIDE):
            sh_copy(blk, zz, 0).wait_recv()
    for yy in range(SIDE):

        @pl.when(my_y == yy)
        def _():
            whole = jnp.concatenate(
                [
                    sh_buf[blk, zz].astype(F32)
                    for blk in range(BLOCKS)
                    for zz in range(SIDE)
                ],
                axis=0,
            )
            sec_out[...] = whole[:, share * yy : share * yy + share].astype(BF16)

    for blk in range(BLOCKS):
        for yo in FAR:
            for zo in FAR:
                dest = ((my_z + zo) % SIDE) * SIDE + (my_y + yo) % SIDE
                if not (yo == 0 and zo == 0):
                    rs_copy(blk, me, dest, my_y, my_z).wait_send()

        @pl.when(sec < last)
        def _():
            for dest in range(team):
                ag_copy(blk, me, dest).wait_send()

        for j in range(SIDE):

            @pl.when(my_y * SIDE + j != me)
            def _():
                sh_copy(blk, my_z, j).wait_send()

    @pl.when(sec == 0)
    def _():
        def sent(j, carry):
            init_copy((me + j) % team).wait_send()
            return carry

        lax.fori_loop(1, team, sent, 0)


def shards(
    hidden_in,
    pre_gain,
    w_zx,
    w_bc,
    w_dt,
    dt_bias,
    a_log,
    d_skip,
    conv_x_weight,
    conv_x_bias,
    conv_bc_weight,
    conv_bc_bias,
    inner_gain,
    w_out,
    conv_x_state,
    conv_bc_state,
    ssm_state,
    sections,
):
    streams, share = hidden_in.shape
    _, heads, p_size, width = w_out.shape
    n2 = w_bc.shape[2]
    n_state = n2 // 2
    team = SIDE * SIDE
    chunk, block = width // SIDE, streams // BLOCKS
    rows = block // SIDE
    hp = heads * p_size
    cols = n2 + 128 * heads + 128
    pairs = (heads + 1) // 2
    args = (
        hidden_in,
        pre_gain,
        jnp.transpose(w_zx[0], (1, 0, 2)),
        w_bc[0],
        jnp.transpose(w_dt[0], (1, 0)),
        dt_bias,
        a_log,
        d_skip,
        jnp.transpose(conv_x_weight[0], (1, 0, 2)),
        jnp.transpose(conv_x_bias, (1, 0, 2)),
        conv_bc_weight[0],
        conv_bc_bias,
        jnp.transpose(inner_gain, (1, 0, 2)),
        w_out[0].reshape(hp, width),
        jnp.transpose(conv_x_state[0], (1, 2, 0, 3)),
        jnp.transpose(conv_bc_state[0], (1, 0, 2)),
        ssm_state[0].reshape(streams, hp, n_state),
    )
    vmem = pl.BlockSpec(memory_space=pltpu.VMEM)
    hbm = pl.BlockSpec(memory_space=pltpu.HBM)
    small = (1, 4, 5, 6, 7, 8, 9, 10, 11, 12, 14, 15)
    dma = pltpu.SemaphoreType.DMA
    sec_new, cx_new, cb_new, ssm_new = pl.pallas_call(
        functools.partial(kernel, sections),
        out_shape=(
            jax.ShapeDtypeStruct((streams, share), BF16),
            jax.ShapeDtypeStruct((3, heads, streams, p_size), BF16),
            jax.ShapeDtypeStruct((3, streams, n2), BF16),
            jax.ShapeDtypeStruct((streams, hp, n_state), BF16),
        ),
        in_specs=[hbm] * len(args),
        out_specs=(vmem, vmem, vmem, vmem),
        scratch_shapes=[pltpu.VMEM(args[i].shape, args[i].dtype) for i in small]
        + [
            pltpu.VMEM((width, cols), BF16),
            pltpu.VMEM((SIDE, hp, chunk), BF16),
            pltpu.VMEM((BLOCKS, SIDE, SIDE, rows, chunk), BF16),
            pltpu.VMEM((block, cols), F32),
            pltpu.VMEM((128, width), F32),
            pltpu.VMEM((streams, n2), F32),
            pltpu.VMEM((pairs, streams, 128), F32),
            pltpu.VMEM((3, pairs, 1, 128), F32),
            pltpu.VMEM((block, 128 * pairs), F32),
            pltpu.VMEM((block, 128 * pairs), BF16),
            pltpu.VMEM((pairs, streams, 128), F32),
            pltpu.VMEM((heads, streams, 128), F32),
            pltpu.VMEM((streams, n_state), F32),
            pltpu.VMEM((pairs, streams, 128), BF16),
            pltpu.VMEM((128 * pairs, 128), F32),
            pltpu.VMEM((BLOCKS, SIDE, SIDE, rows, chunk + 128), BF16),
            pltpu.VMEM((BLOCKS, team, rows, chunk + 128), BF16),
            pltpu.VMEM((BLOCKS, rows, chunk), BF16),
            pltpu.VMEM((team, streams, share), BF16),
            pltpu.VMEM((BLOCKS, SIDE, rows, chunk), BF16),
            dma((1 + heads + SIDE + 1,)),
            dma((len(small),)),
            dma((team,)),
            dma((team,)),
            dma((BLOCKS, team)),
            dma((BLOCKS, team)),
            dma((BLOCKS, team)),
            dma((BLOCKS, team)),
            dma((BLOCKS, SIDE)),
            dma((BLOCKS, SIDE)),
        ],
        compiler_params=pltpu.CompilerParams(
            collective_id=0, has_side_effects=True, vmem_limit_bytes=40 * 1024 * 1024
        ),
        name="stack_step",
    )(*[pltpu.with_memory_space_constraint(a, pltpu.HBM) for a in args])
    return (
        sec_new[None],
        jnp.transpose(cx_new, (2, 0, 1, 3))[None],
        jnp.transpose(cb_new, (1, 0, 2))[None],
        ssm_new.reshape(ssm_state.shape),
    )


def solution(mesh):
    placed = (
        P(None, "tensor"),
        P("section", None),
        P("section", None, "tensor", None),
        P("section", None, None),
        P("section", None, "tensor"),
        P("section", "tensor"),
        P("section", "tensor"),
        P("section", "tensor"),
        P("section", None, "tensor", None),
        P("section", "tensor", None),
        P("section", None, None),
        P("section", None),
        P("section", "tensor", None),
        P("section", "tensor", None, None),
        P("section", None, None, "tensor", None),
        P("section", None, None, None),
        P("section", None, "tensor", None, None),
    )
    return jax.shard_map(
        functools.partial(shards, sections=mesh.shape["section"]),
        mesh=mesh,
        in_specs=placed,
        out_specs=(
            P("section", None, "tensor"),
            P("section", None, None, "tensor", None),
            P("section", None, None, None),
            P("section", None, "tensor", None, None),
        ),
        check_vma=False,
    )
```

```python
import functools

import jax
import jax.numpy as jnp
from jax import lax
from jax.experimental import pallas as pl
from jax.experimental.pallas import tpu as pltpu
from jax.sharding import PartitionSpec as P

epsilon = 1e-05
MESH = pl.DeviceIdType.MESH
F32, BF16 = jnp.float32, jnp.bfloat16
SIDE = 4
NEAR = (0, 1, 3, 2)
FAR = (2, 1, 3, 0)
PIECES = 4
BLOCKS = 2
EARLY = (1, 3)


def silu(v):
    return v / (1.0 + jnp.exp(-v))


def softplus(v):
    return jnp.maximum(v, 0.0) + jnp.log1p(jnp.exp(-jnp.abs(v)))


def kernel(
    sections,
    hid_hbm,
    gain_hbm,
    wzx_hbm,
    wbc_hbm,
    wdt_hbm,
    dtb_hbm,
    alog_hbm,
    dsk_hbm,
    cxw_hbm,
    cxb_hbm,
    cbw_hbm,
    cbb_hbm,
    ig_hbm,
    wout_hbm,
    cxs_hbm,
    cbs_hbm,
    ssm_hbm,
    sec_out,
    cx_out,
    cb_out,
    st,
    hid_ref,
    pack,
    gain_ref,
    wdt_ref,
    dtb_ref,
    alog_ref,
    dsk_ref,
    cxw_ref,
    cxb_ref,
    cbw_ref,
    cbb_ref,
    ig_ref,
    cxs_ref,
    cbs_ref,
    w_all,
    w_o,
    hbuf,
    acc,
    wdt_pad,
    pre_bc,
    pre_x,
    par,
    q_buf,
    inner,
    stx,
    dec,
    b_buf,
    xf_buf,
    stx_t,
    send_buf,
    rs_buf,
    ag_src,
    init_buf,
    sh_buf,
    hid_sem,
    load_sem,
    small_sem,
    init_send,
    init_recv,
    rs_send,
    rs_recv,
    ag_send,
    ag_recv,
    sh_send,
    sh_recv,
):
    heads, streams, p_size = cxs_hbm.shape[1:]
    width, n2 = wbc_hbm.shape
    n_state = n2 // 2
    chunk = width // SIDE
    block = streams // BLOCKS
    rows = block // SIDE
    share = hid_hbm.shape[1]
    team = SIDE * SIDE
    last = sections - 1

    sec = lax.axis_index("section")
    me = lax.axis_index("tensor")
    my_z = me // SIDE
    my_y = me % SIDE

    def dev(s, t):
        return {"section": s, "tensor": t}

    loads = [pltpu.make_async_copy(wbc_hbm, w_all.at[:, pl.ds(0, n2)], load_sem.at[0])]
    for h in range(heads):
        loads.append(
            pltpu.make_async_copy(
                wzx_hbm.at[h], w_all.at[:, pl.ds(n2 + 128 * h, 128)], load_sem.at[1 + h]
            )
        )
    at = 1 + heads
    for yy in range(SIDE):
        loads.append(
            pltpu.make_async_copy(
                wout_hbm.at[:, pl.ds(chunk * yy, chunk)], w_o.at[yy], load_sem.at[at + yy]
            )
        )
    at += SIDE
    loads.append(pltpu.make_async_copy(ssm_hbm, st, load_sem.at[at]))
    smalls = [
        pltpu.make_async_copy(a, b, small_sem.at[i])
        for i, (a, b) in enumerate(
            (
                (wdt_hbm, wdt_ref),
                (gain_hbm, gain_ref),
                (dtb_hbm, dtb_ref),
                (alog_hbm, alog_ref),
                (dsk_hbm, dsk_ref),
                (cxw_hbm, cxw_ref),
                (cxb_hbm, cxb_ref),
                (cbw_hbm, cbw_ref),
                (cbb_hbm, cbb_ref),
                (ig_hbm, ig_ref),
                (cxs_hbm, cxs_ref),
                (cbs_hbm, cbs_ref),
            )
        )
    ]

    barrier = pltpu.get_barrier_semaphore()

    ring = [
        ((my_z + zo) % SIDE) * SIDE + (my_y + yo) % SIDE for yo in FAR for zo in FAR
    ]

    for other in ring[:-1]:
        pl.semaphore_signal(barrier, inc=1, device_id=dev(sec, other), device_id_type=MESH)

    @pl.when(sec > 0)
    def _():
        for other in ring:
            pl.semaphore_signal(barrier, inc=1, device_id=dev(sec - 1, other), device_id_type=MESH)

    @pl.when(sec < last)
    def _():
        for other in ring:
            pl.semaphore_signal(barrier, inc=1, device_id=dev(sec + 1, other), device_id_type=MESH)

    hid_copy = pltpu.make_async_copy(hid_hbm, hid_ref, hid_sem)
    hid_copy.start()
    for cp in smalls + loads:
        cp.start()

    hid_copy.wait()
    for blk in range(BLOCKS):
        parts = [
            hid_ref[blk * block + rows * zz : blk * block + rows * zz + rows, :].astype(F32)
            if rows % 16 == 0
            else hid_ref[blk * block : blk * block + block, :].astype(F32)[rows * zz : rows * zz + rows]
            for zz in range(SIDE)
        ]
        pack[blk] = jnp.concatenate(parts, axis=1).astype(BF16)

    partners = team - 1 + jnp.where(sec > 0, team, 0) + jnp.where(sec < last, team, 0)
    pl.semaphore_wait(barrier, partners)

    def init_copy(blk, src_t, dest):
        return pltpu.make_async_remote_copy(
            src_ref=pack.at[blk],
            dst_ref=init_buf.at[blk, src_t],
            send_sem=init_send.at[blk, dest],
            recv_sem=init_recv.at[blk, src_t],
            device_id=dev(sec, dest),
            device_id_type=MESH,
        )

    def init_own(blk):
        return pltpu.make_async_copy(
            pack.at[blk], init_buf.at[blk, me], init_recv.at[blk, me]
        )

    @pl.when(sec == 0)
    def _():
        for blk in range(BLOCKS):
            for other in ring[:-1]:
                init_copy(blk, me, other).start()
            init_own(blk).start()

    for cp in smalls:
        cp.wait()
    wdt_pad[...] = jnp.zeros_like(wdt_pad)
    wdt_pad[0:heads, :] = wdt_ref[...].astype(F32)
    for h in range(1 + heads):
        loads[h].wait()
    for j in range(width // 128):
        blk = wdt_pad[:, 128 * j : 128 * j + 128]
        w_all[128 * j : 128 * j + 128, n2 + 128 * heads : n2 + 128 * heads + 128] = blk.T.astype(BF16)
    q_buf[...] = jnp.zeros_like(q_buf)
    cb_out[0] = cbs_ref[1]
    cb_out[1] = cbs_ref[2]
    cx_out[0] = cxs_ref[1]
    cx_out[1] = cxs_ref[2]
    cbw = cbw_ref[...]
    pre_bc[...] = (
        cbs_ref[0].astype(F32) * cbw[0:1]
        + cbs_ref[1].astype(F32) * cbw[1:2]
        + cbs_ref[2].astype(F32) * cbw[2:3]
        + cbb_ref[...]
    )
    pairs = (heads + 1) // 2

    def packed(get, k):
        a = get(2 * k)
        b = get(2 * k + 1) if 2 * k + 1 < heads else jnp.zeros_like(a)
        return jnp.concatenate([a, b], axis=1)

    def pre_of(h):
        w = cxw_ref[h]
        return (
            cxs_ref[0, h].astype(F32) * w[0:1]
            + cxs_ref[1, h].astype(F32) * w[1:2]
            + cxs_ref[2, h].astype(F32) * w[2:3]
            + cxb_ref[h]
        )

    for k in range(pairs):
        pre_x[k] = packed(pre_of, k)
        par[0, k] = packed(lambda h: cxw_ref[h][3:4], k)
        par[1, k] = packed(lambda h: ig_ref[h], k)
        par[2, k] = packed(
            lambda h: jnp.broadcast_to(dsk_ref[:, h : h + 1], (1, p_size)), k
        )
    pad = jnp.zeros((1, 128 - heads), F32)
    dtb = jnp.concatenate([dtb_ref[...], pad], axis=1)
    neg_a = -jnp.exp(jnp.concatenate([alog_ref[...], pad], axis=1))

    def ag_copy(blk, src_t, dest):
        return pltpu.make_async_remote_copy(
            src_ref=ag_src.at[blk],
            dst_ref=hbuf.at[blk, src_t % SIDE, src_t // SIDE],
            send_sem=ag_send.at[blk, dest],
            recv_sem=ag_recv.at[blk, src_t],
            device_id=dev(jnp.minimum(sec + 1, last), dest),
            device_id_type=MESH,
        )

    def rs_copy(blk, src_t, dest, yy, zz):
        return pltpu.make_async_remote_copy(
            src_ref=send_buf.at[blk, yy, zz],
            dst_ref=rs_buf.at[blk, src_t],
            send_sem=rs_send.at[blk, dest],
            recv_sem=rs_recv.at[blk, src_t],
            device_id=dev(sec, dest),
            device_id_type=MESH,
        )

    def rs_own(blk):
        return pltpu.make_async_copy(
            send_buf.at[blk, my_y, my_z], rs_buf.at[blk, me], rs_recv.at[blk, me]
        )

    for cp in loads[1 + heads :]:
        cp.wait()
    lane = lax.broadcasted_iota(jnp.int32, (block, 128), 1)
    low = lane < p_size
    hp = heads * p_size
    dt0 = n2 + 128 * heads
    group = 16
    row = lax.broadcasted_iota(jnp.int32, (group, n_state), 0)

    def layer(blk, carry):
        here = pl.ds(pl.multiple_of(blk * block, block), block)

        @pl.when(sec == 0)
        def _():
            for other in ring[:-1]:
                init_copy(blk, other, me).wait_recv()
            init_own(blk).wait()
            for yy in range(SIDE):
                parts = [init_buf[blk, SIDE * yy + i].astype(F32) for i in range(SIDE)]
                for zz in range(SIDE):
                    hbuf[blk, yy, zz] = jnp.concatenate(
                        [part[:, share * zz : share * zz + share] for part in parts], axis=1
                    ).astype(BF16)

        sq = jnp.zeros((block, 128), F32)
        for off in NEAR:
            yy = (my_y + off) % SIDE

            @pl.when(sec > 0)
            def _():
                for zo in NEAR:
                    ag_copy(blk, ((my_z + zo) % SIDE) * SIDE + yy, me).wait_recv()

            hv = jnp.concatenate([hbuf[blk, yy, zz].astype(F32) for zz in range(SIDE)], axis=0)
            for i in range(chunk // 128):
                part = hv[:, 128 * i : 128 * i + 128]
                sq = sq + part * part
            start = pl.multiple_of(yy * chunk, chunk)
            hg = (hv * gain_ref[:, pl.ds(start, chunk)]).astype(BF16)
            term = jnp.dot(hg, w_all[pl.ds(start, chunk), :], preferred_element_type=F32)
            if off == NEAR[0]:
                acc[...] = term
            else:
                acc[...] += term
        r = lax.rsqrt(jnp.sum(sq, axis=1, keepdims=True) * (1.0 / width) + epsilon)

        bcf = (acc[:, 0:n2] * r).astype(BF16)
        cb_out[2, here, :] = bcf
        bcv = silu(pre_bc[here, :] + bcf.astype(F32) * cbw_ref[3:4, :])
        b_in = bcv[:, 0:n_state]
        c_out = bcv[:, n_state:n2]
        b_buf[here, :] = b_in
        bd = jnp.sum(b_in * c_out, axis=1, keepdims=True)

        for g in range(block // group):
            c16 = c_out[group * g : group * g + group]
            base = blk * block + group * g
            total = None
            for i in range(0, group, 2):
                lhs = jnp.concatenate(
                    [jnp.where(row == i, c16, 0.0), jnp.where(row == i + 1, c16, 0.0)], axis=1
                ).astype(BF16)
                rhs = jnp.concatenate([st[base + i], st[base + i + 1]], axis=1)
                term = lax.dot_general(
                    lhs, rhs, (((1,), (1,)), ((), ())), preferred_element_type=F32
                )
                total = term if total is None else total + term
            q_buf[group * g : group * g + group, 0:hp] = total

        step = softplus(acc[:, dt0 : dt0 + 128] * r + dtb)
        decay = jnp.exp(step * neg_a)

        def each(v):
            return [jnp.broadcast_to(v[:, h : h + 1], (block, 128)) for h in range(heads)]

        steps, decays = each(step), each(decay)
        for h in range(heads):
            dec[h, here, :] = decays[h]

        def spread(v, k):
            return jnp.where(low, v[2 * k], v[min(2 * k + 1, heads - 1)])

        sq = jnp.zeros((block, 128), F32)
        for k in range(pairs):
            a = acc[:, n2 + 256 * k : n2 + 256 * k + 128]
            if 2 * k + 1 < heads:
                b = acc[:, n2 + 256 * k + 128 : n2 + 256 * k + 256]
            else:
                b = jnp.zeros_like(a)
            x_new = jnp.where(low, pltpu.roll(a, p_size, 1), b)
            z_new = jnp.where(low, a, pltpu.roll(b, p_size, 1))
            xf = (x_new * r).astype(BF16)
            xf_buf[k, here, :] = xf
            xc = silu(pre_x[k, here, :] + xf.astype(F32) * par[0, k])
            sx = spread(steps, k) * xc
            stx[k, here, :] = sx
            q = q_buf[:, 128 * k : 128 * k + 128]
            y_out = spread(decays, k) * q + sx * bd + par[2, k] * xc
            gated = y_out * silu(z_new * r)
            sq = sq + gated * gated
            inner[:, 128 * k : 128 * k + 128] = (gated * par[1, k]).astype(BF16)
        squares = jnp.sum(sq, axis=1, keepdims=True)
        hi = squares.astype(BF16).astype(F32)
        lo = squares - hi
        sq_tile = jnp.where(lane == 0, hi, jnp.where(lane == 1, lo, 0.0))

        for yo in FAR:
            yy = (my_y + yo) % SIDE
            part = jnp.dot(inner[:, 0:hp], w_o[yy], preferred_element_type=F32)
            whole = jnp.concatenate([part, sq_tile], axis=1)
            for zz in range(SIDE):
                send_buf[blk, yy, zz] = whole[rows * zz : rows * zz + rows].astype(BF16)
            for zo in FAR:
                zz = (my_z + zo) % SIDE
                if yo == 0 and zo == 0:
                    rs_own(blk).start()
                else:
                    rs_copy(blk, me, zz * SIDE + yy, yy, zz).start()
        return carry

    lax.fori_loop(0, BLOCKS, layer, 0)

    octet = 8
    per_block = block // octet

    def turn():
        zeros = jnp.zeros((128 - streams, 128), F32)
        for k in range(pairs):
            stx_t[128 * k : 128 * k + 128] = jnp.concatenate([stx[k], zeros], axis=0).T

    def update(g, carry):
        shift = (128 - g * octet) % 128
        span8 = pl.ds(pl.multiple_of(g * octet, octet), octet)
        b8 = b_buf[span8, :]
        for h in range(heads):
            span = slice(p_size * h, p_size * h + p_size)
            sx_r = pltpu.roll(stx_t[span, :], shift, 1)
            d8 = dec[h, span8, :]
            for i in range(octet):
                old = st[g * octet + i, span, :].astype(F32)
                new = d8[i : i + 1] * old + jnp.broadcast_to(
                    sx_r[:, i : i + 1], (p_size, 128)
                ) * b8[i : i + 1]
                st[g * octet + i, span, :] = new.astype(BF16)
        return carry

    def sh_copy(blk, src_z, j):
        return pltpu.make_async_remote_copy(
            src_ref=ag_src.at[blk],
            dst_ref=sh_buf.at[blk, src_z],
            send_sem=sh_send.at[blk, j],
            recv_sem=sh_recv.at[blk, src_z],
            device_id=dev(sec, my_y * SIDE + j),
            device_id_type=MESH,
        )

    turn()
    for blk in range(BLOCKS):
        lax.fori_loop(EARLY[blk - 1] if blk else 0, EARLY[blk], update, 0)

        tot = jnp.zeros((rows, chunk + 128), F32)
        for yo in NEAR:
            for zo in NEAR:
                src = ((my_z + zo) % SIDE) * SIDE + (my_y + yo) % SIDE
                if yo == 0 and zo == 0:
                    rs_own(blk).wait()
                else:
                    rs_copy(blk, src, me, my_y, my_z).wait_recv()
                tot = tot + rs_buf[blk, src].astype(F32)
        scale = lax.rsqrt(
            jnp.sum(tot[:, chunk : chunk + 128], axis=1, keepdims=True) * (1.0 / (hp * team))
            + epsilon
        )
        mine = hbuf[blk, my_y, my_z].astype(F32)
        ag_src[blk] = (mine + tot[:, 0:chunk] * scale).astype(BF16)

        @pl.when(sec < last)
        def _():
            for yo in FAR:
                for zo in FAR:
                    ag_copy(blk, me, ((my_z + zo) % SIDE) * SIDE + (my_y + yo) % SIDE).start()

        for j in range(SIDE):
            own = my_y * SIDE + j == me

            @pl.when(own)
            def _():
                pltpu.make_async_copy(
                    ag_src.at[blk], sh_buf.at[blk, my_z], sh_recv.at[blk, my_z]
                ).start()

            @pl.when(jnp.logical_not(own))
            def _():
                sh_copy(blk, my_z, j).start()

    lax.fori_loop(EARLY[-1], streams // octet, update, 0)

    for h in range(heads):
        xf = xf_buf[h // 2].astype(F32)
        cx_out[2, h] = xf[:, p_size * (h % 2) : p_size * (h % 2) + p_size].astype(BF16)

    for blk in range(BLOCKS):
        for zz in range(SIDE):
            sh_copy(blk, zz, 0).wait_recv()
    for yy in range(SIDE):

        @pl.when(my_y == yy)
        def _():
            whole = jnp.concatenate(
                [
                    sh_buf[blk, zz].astype(F32)
                    for blk in range(BLOCKS)
                    for zz in range(SIDE)
                ],
                axis=0,
            )
            sec_out[...] = whole[:, share * yy : share * yy + share].astype(BF16)

    for blk in range(BLOCKS):
        for yo in FAR:
            for zo in FAR:
                dest = ((my_z + zo) % SIDE) * SIDE + (my_y + yo) % SIDE
                if not (yo == 0 and zo == 0):
                    rs_copy(blk, me, dest, my_y, my_z).wait_send()

        @pl.when(sec < last)
        def _():
            for dest in range(team):
                ag_copy(blk, me, dest).wait_send()

        for j in range(SIDE):

            @pl.when(my_y * SIDE + j != me)
            def _():
                sh_copy(blk, my_z, j).wait_send()

    @pl.when(sec == 0)
    def _():
        for blk in range(BLOCKS):
            for other in ring[:-1]:
                init_copy(blk, me, other).wait_send()


def write_out(a_in, b_in, c_in, d_in, a_out, b_out, c_out, d_out, sems):
    size = d_in.shape[0] // PIECES
    copies = [
        pltpu.make_async_copy(d_in.at[pl.ds(size * i, size)], d_out.at[pl.ds(size * i, size)], sems.at[3 + i])
        for i in range(PIECES)
    ]
    for i, (x, y) in enumerate(((a_in, a_out), (b_in, b_out), (c_in, c_out))):
        copies.append(pltpu.make_async_copy(x, y, sems.at[i]))
    for cp in copies:
        cp.start()
    for cp in copies:
        cp.wait()


def shards(
    hidden_in,
    pre_gain,
    w_zx,
    w_bc,
    w_dt,
    dt_bias,
    a_log,
    d_skip,
    conv_x_weight,
    conv_x_bias,
    conv_bc_weight,
    conv_bc_bias,
    inner_gain,
    w_out,
    conv_x_state,
    conv_bc_state,
    ssm_state,
    sections,
):
    streams, share = hidden_in.shape
    _, heads, p_size, width = w_out.shape
    n2 = w_bc.shape[2]
    n_state = n2 // 2
    team = SIDE * SIDE
    chunk, block = width // SIDE, streams // BLOCKS
    rows = block // SIDE
    hp = heads * p_size
    cols = n2 + 128 * heads + 128
    pairs = (heads + 1) // 2
    args = (
        hidden_in,
        pre_gain,
        jnp.transpose(w_zx[0], (1, 0, 2)),
        w_bc[0],
        jnp.transpose(w_dt[0], (1, 0)),
        dt_bias,
        a_log,
        d_skip,
        jnp.transpose(conv_x_weight[0], (1, 0, 2)),
        jnp.transpose(conv_x_bias, (1, 0, 2)),
        conv_bc_weight[0],
        conv_bc_bias,
        jnp.transpose(inner_gain, (1, 0, 2)),
        w_out[0].reshape(hp, width),
        jnp.transpose(conv_x_state[0], (1, 2, 0, 3)),
        jnp.transpose(conv_bc_state[0], (1, 0, 2)),
        ssm_state[0].reshape(streams, hp, n_state),
    )
    vmem = pl.BlockSpec(memory_space=pltpu.VMEM)
    hbm = pl.BlockSpec(memory_space=pltpu.HBM)
    small = (1, 4, 5, 6, 7, 8, 9, 10, 11, 12, 14, 15)
    dma = pltpu.SemaphoreType.DMA
    sec_new, cx_new, cb_new, ssm_new = pl.pallas_call(
        functools.partial(kernel, sections),
        out_shape=(
            jax.ShapeDtypeStruct((streams, share), BF16),
            jax.ShapeDtypeStruct((3, heads, streams, p_size), BF16),
            jax.ShapeDtypeStruct((3, streams, n2), BF16),
            jax.ShapeDtypeStruct((streams, hp, n_state), BF16),
        ),
        in_specs=[hbm] * len(args),
        out_specs=(vmem, vmem, vmem, vmem),
        scratch_shapes=[
            pltpu.VMEM((streams, share), BF16),
            pltpu.VMEM((BLOCKS, rows, chunk), BF16),
        ]
        + [pltpu.VMEM(args[i].shape, args[i].dtype) for i in small]
        + [
            pltpu.VMEM((width, cols), BF16),
            pltpu.VMEM((SIDE, hp, chunk), BF16),
            pltpu.VMEM((BLOCKS, SIDE, SIDE, rows, chunk), BF16),
            pltpu.VMEM((block, cols), F32),
            pltpu.VMEM((128, width), F32),
            pltpu.VMEM((streams, n2), F32),
            pltpu.VMEM((pairs, streams, 128), F32),
            pltpu.VMEM((3, pairs, 1, 128), F32),
            pltpu.VMEM((block, 128 * pairs), F32),
            pltpu.VMEM((block, 128 * pairs), BF16),
            pltpu.VMEM((pairs, streams, 128), F32),
            pltpu.VMEM((heads, streams, 128), F32),
            pltpu.VMEM((streams, n_state), F32),
            pltpu.VMEM((pairs, streams, 128), BF16),
            pltpu.VMEM((128 * pairs, 128), F32),
            pltpu.VMEM((BLOCKS, SIDE, SIDE, rows, chunk + 128), BF16),
            pltpu.VMEM((BLOCKS, team, rows, chunk + 128), BF16),
            pltpu.VMEM((BLOCKS, rows, chunk), BF16),
            pltpu.VMEM((BLOCKS, team, rows, chunk), BF16),
            pltpu.VMEM((BLOCKS, SIDE, rows, chunk), BF16),
            dma(()),
            dma((1 + heads + SIDE + 1,)),
            dma((len(small),)),
            dma((BLOCKS, team)),
            dma((BLOCKS, team)),
            dma((BLOCKS, team)),
            dma((BLOCKS, team)),
            dma((BLOCKS, team)),
            dma((BLOCKS, team)),
            dma((BLOCKS, SIDE)),
            dma((BLOCKS, SIDE)),
        ],
        compiler_params=pltpu.CompilerParams(
            collective_id=0, has_side_effects=True, vmem_limit_bytes=40 * 1024 * 1024
        ),
        name="stack_step",
    )(*[pltpu.with_memory_space_constraint(a, pltpu.HBM) for a in args])
    results = (sec_new, cx_new, cb_new, ssm_new)
    sec_new, cx_new, cb_new, ssm_new = pl.pallas_call(
        write_out,
        out_shape=tuple(jax.ShapeDtypeStruct(a.shape, a.dtype) for a in results),
        in_specs=[vmem] * 4,
        out_specs=(pl.BlockSpec(memory_space=pltpu.HBM),) * 4,
        scratch_shapes=[dma((3 + PIECES,))],
        compiler_params=pltpu.CompilerParams(vmem_limit_bytes=16 * 1024 * 1024),
        name="write_out",
    )(*results)
    return (
        sec_new[None],
        jnp.transpose(cx_new, (2, 0, 1, 3))[None],
        jnp.transpose(cb_new, (1, 0, 2))[None],
        ssm_new.reshape(ssm_state.shape),
    )


def solution(mesh):
    placed = (
        P(None, "tensor"),
        P("section", None),
        P("section", None, "tensor", None),
        P("section", None, None),
        P("section", None, "tensor"),
        P("section", "tensor"),
        P("section", "tensor"),
        P("section", "tensor"),
        P("section", None, "tensor", None),
        P("section", "tensor", None),
        P("section", None, None),
        P("section", None),
        P("section", "tensor", None),
        P("section", "tensor", None, None),
        P("section", None, None, "tensor", None),
        P("section", None, None, None),
        P("section", None, "tensor", None, None),
    )
    return jax.shard_map(
        functools.partial(shards, sections=mesh.shape["section"]),
        mesh=mesh,
        in_specs=placed,
        out_specs=(
            P("section", None, "tensor"),
            P("section", None, None, "tensor", None),
            P("section", None, None, None),
            P("section", None, "tensor", None, None),
        ),
        check_vma=False,
    )
```

```python
import functools

import jax
import jax.numpy as jnp
from jax import lax
from jax.experimental import pallas as pl
from jax.experimental.pallas import tpu as pltpu
from jax.sharding import PartitionSpec as P

epsilon = 1e-05
MESH = pl.DeviceIdType.MESH
F32, BF16 = jnp.float32, jnp.bfloat16
SIDE = 4
NEAR = (0, 1, 3, 2)
FAR = (2, 1, 3, 0)
PIECES = 4
BLOCKS = 2
EARLY = (2, 6)


def silu(v):
    return v / (1.0 + jnp.exp(-v))


def softplus(v):
    return jnp.maximum(v, 0.0) + jnp.log1p(jnp.exp(-jnp.abs(v)))


def kernel(
    sections,
    hid_hbm,
    gain_hbm,
    wzx_hbm,
    wbc_hbm,
    wdt_hbm,
    dtb_hbm,
    alog_hbm,
    dsk_hbm,
    cxw_hbm,
    cxb_hbm,
    cbw_hbm,
    cbb_hbm,
    ig_hbm,
    wout_hbm,
    cxs_hbm,
    cbs_hbm,
    ssm_hbm,
    sec_out,
    cx_out,
    cb_out,
    st,
    hid_ref,
    pack,
    gain_ref,
    wdt_ref,
    dtb_ref,
    alog_ref,
    dsk_ref,
    cxw_ref,
    cxb_ref,
    cbw_ref,
    cbb_ref,
    ig_ref,
    cxs_ref,
    cbs_ref,
    w_all,
    w_o,
    hbuf,
    acc,
    wdt_pad,
    pre_bc,
    pre_x,
    par,
    q_buf,
    inner,
    stx,
    dec,
    b_buf,
    xf_buf,
    stx_t,
    send_buf,
    rs_buf,
    ag_src,
    init_buf,
    sh_buf,
    send_end,
    sum_end,
    end_buf,
    hid_sem,
    load_sem,
    small_sem,
    init_send,
    init_recv,
    rs_send,
    rs_recv,
    ag_send,
    ag_recv,
    sh_send,
    sh_recv,
):
    heads, streams, p_size = cxs_hbm.shape[1:]
    width, n2 = wbc_hbm.shape
    n_state = n2 // 2
    chunk = width // SIDE
    block = streams // BLOCKS
    rows = block // SIDE
    share = hid_hbm.shape[1]
    team = SIDE * SIDE
    last = sections - 1

    sec = lax.axis_index("section")
    me = lax.axis_index("tensor")
    my_z = me // SIDE
    my_y = me % SIDE

    def dev(s, t):
        return {"section": s, "tensor": t}

    loads = [pltpu.make_async_copy(wbc_hbm, w_all.at[:, pl.ds(0, n2)], load_sem.at[0])]
    for h in range(heads):
        loads.append(
            pltpu.make_async_copy(
                wzx_hbm.at[h], w_all.at[:, pl.ds(n2 + 128 * h, 128)], load_sem.at[1 + h]
            )
        )
    at = 1 + heads
    for yy in range(SIDE):
        loads.append(
            pltpu.make_async_copy(
                wout_hbm.at[:, pl.ds(chunk * yy, chunk)], w_o.at[yy], load_sem.at[at + yy]
            )
        )
    at += SIDE
    loads.append(pltpu.make_async_copy(ssm_hbm, st, load_sem.at[at]))
    smalls = [
        pltpu.make_async_copy(a, b, small_sem.at[i])
        for i, (a, b) in enumerate(
            (
                (wdt_hbm, wdt_ref),
                (gain_hbm, gain_ref),
                (dtb_hbm, dtb_ref),
                (alog_hbm, alog_ref),
                (dsk_hbm, dsk_ref),
                (cxw_hbm, cxw_ref),
                (cxb_hbm, cxb_ref),
                (cbw_hbm, cbw_ref),
                (cbb_hbm, cbb_ref),
                (ig_hbm, ig_ref),
                (cxs_hbm, cxs_ref),
                (cbs_hbm, cbs_ref),
            )
        )
    ]

    barrier = pltpu.get_barrier_semaphore()

    ring = [
        ((my_z + zo) % SIDE) * SIDE + (my_y + yo) % SIDE for yo in FAR for zo in FAR
    ]

    for other in ring[:-1]:
        pl.semaphore_signal(barrier, inc=1, device_id=dev(sec, other), device_id_type=MESH)

    @pl.when(sec > 0)
    def _():
        for other in ring:
            pl.semaphore_signal(barrier, inc=1, device_id=dev(sec - 1, other), device_id_type=MESH)

    @pl.when(sec < last)
    def _():
        for other in ring:
            pl.semaphore_signal(barrier, inc=1, device_id=dev(sec + 1, other), device_id_type=MESH)

    hid_copy = pltpu.make_async_copy(hid_hbm, hid_ref, hid_sem)
    hid_copy.start()
    for cp in smalls + loads:
        cp.start()

    hid_copy.wait()
    for blk in range(BLOCKS):
        parts = [
            hid_ref[blk * block + rows * zz : blk * block + rows * zz + rows, :].astype(F32)
            if rows % 16 == 0
            else hid_ref[blk * block : blk * block + block, :].astype(F32)[rows * zz : rows * zz + rows]
            for zz in range(SIDE)
        ]
        pack[blk] = jnp.concatenate(parts, axis=1).astype(BF16)

    partners = team - 1 + jnp.where(sec > 0, team, 0) + jnp.where(sec < last, team, 0)
    pl.semaphore_wait(barrier, partners)

    def init_copy(blk, src_t, dest):
        return pltpu.make_async_remote_copy(
            src_ref=pack.at[blk],
            dst_ref=init_buf.at[blk, src_t],
            send_sem=init_send.at[blk, dest],
            recv_sem=init_recv.at[blk, src_t],
            device_id=dev(sec, dest),
            device_id_type=MESH,
        )

    def init_own(blk):
        return pltpu.make_async_copy(
            pack.at[blk], init_buf.at[blk, me], init_recv.at[blk, me]
        )

    @pl.when(sec == 0)
    def _():
        for blk in range(BLOCKS):
            for other in ring[:-1]:
                init_copy(blk, me, other).start()
            init_own(blk).start()

    for cp in smalls:
        cp.wait()
    wdt_pad[...] = jnp.zeros_like(wdt_pad)
    wdt_pad[0:heads, :] = wdt_ref[...].astype(F32)
    for h in range(1 + heads):
        loads[h].wait()
    for j in range(width // 128):
        blk = wdt_pad[:, 128 * j : 128 * j + 128]
        w_all[128 * j : 128 * j + 128, n2 + 128 * heads : n2 + 128 * heads + 128] = blk.T.astype(BF16)
    q_buf[...] = jnp.zeros_like(q_buf)
    cb_out[0] = cbs_ref[1]
    cb_out[1] = cbs_ref[2]
    cx_out[0] = cxs_ref[1]
    cx_out[1] = cxs_ref[2]
    cbw = cbw_ref[...]
    pre_bc[...] = (
        cbs_ref[0].astype(F32) * cbw[0:1]
        + cbs_ref[1].astype(F32) * cbw[1:2]
        + cbs_ref[2].astype(F32) * cbw[2:3]
        + cbb_ref[...]
    )
    pairs = (heads + 1) // 2

    def packed(get, k):
        a = get(2 * k)
        b = get(2 * k + 1) if 2 * k + 1 < heads else jnp.zeros_like(a)
        return jnp.concatenate([a, b], axis=1)

    def pre_of(h):
        w = cxw_ref[h]
        return (
            cxs_ref[0, h].astype(F32) * w[0:1]
            + cxs_ref[1, h].astype(F32) * w[1:2]
            + cxs_ref[2, h].astype(F32) * w[2:3]
            + cxb_ref[h]
        )

    for k in range(pairs):
        pre_x[k] = packed(pre_of, k)
        par[0, k] = packed(lambda h: cxw_ref[h][3:4], k)
        par[1, k] = packed(lambda h: ig_ref[h], k)
        par[2, k] = packed(
            lambda h: jnp.broadcast_to(dsk_ref[:, h : h + 1], (1, p_size)), k
        )
    pad = jnp.zeros((1, 128 - heads), F32)
    dtb = jnp.concatenate([dtb_ref[...], pad], axis=1)
    neg_a = -jnp.exp(jnp.concatenate([alog_ref[...], pad], axis=1))

    def ag_copy(blk, src_t, dest):
        return pltpu.make_async_remote_copy(
            src_ref=ag_src.at[blk],
            dst_ref=hbuf.at[blk, src_t % SIDE, src_t // SIDE],
            send_sem=ag_send.at[blk, dest],
            recv_sem=ag_recv.at[blk, src_t],
            device_id=dev(jnp.minimum(sec + 1, last), dest),
            device_id_type=MESH,
        )

    def rs_copy(blk, src_t, dest, yy, zz):
        return pltpu.make_async_remote_copy(
            src_ref=send_buf.at[blk, yy, zz],
            dst_ref=rs_buf.at[blk, src_t],
            send_sem=rs_send.at[blk, dest],
            recv_sem=rs_recv.at[blk, src_t],
            device_id=dev(sec, dest),
            device_id_type=MESH,
        )

    def rs_own(blk):
        return pltpu.make_async_copy(
            send_buf.at[blk, my_y, my_z], rs_buf.at[blk, me], rs_recv.at[blk, me]
        )

    def end_copy(blk, src_t, zz, j):
        return pltpu.make_async_remote_copy(
            src_ref=send_end.at[blk, zz, j],
            dst_ref=sum_end.at[blk, src_t],
            send_sem=rs_send.at[blk, zz * SIDE + j],
            recv_sem=rs_recv.at[blk, src_t],
            device_id=dev(sec, zz * SIDE + j),
            device_id_type=MESH,
        )

    def end_own(blk):
        return pltpu.make_async_copy(
            send_end.at[blk, my_z, my_y], sum_end.at[blk, me], rs_recv.at[blk, me]
        )

    for cp in loads[1 + heads :]:
        cp.wait()
    lane = lax.broadcasted_iota(jnp.int32, (block, 128), 1)
    low = lane < p_size
    hp = heads * p_size
    dt0 = n2 + 128 * heads
    group = 16
    row = lax.broadcasted_iota(jnp.int32, (group, n_state), 0)

    def layer(blk, carry):
        here = pl.ds(pl.multiple_of(blk * block, block), block)

        @pl.when(sec == 0)
        def _():
            for other in ring[:-1]:
                init_copy(blk, other, me).wait_recv()
            init_own(blk).wait()
            for yy in range(SIDE):
                parts = [init_buf[blk, SIDE * yy + i].astype(F32) for i in range(SIDE)]
                for zz in range(SIDE):
                    hbuf[blk, yy, zz] = jnp.concatenate(
                        [part[:, share * zz : share * zz + share] for part in parts], axis=1
                    ).astype(BF16)

        sq = jnp.zeros((block, 128), F32)
        for off in NEAR:
            yy = (my_y + off) % SIDE

            @pl.when(sec > 0)
            def _():
                for zo in NEAR:
                    ag_copy(blk, ((my_z + zo) % SIDE) * SIDE + yy, me).wait_recv()

            hv = jnp.concatenate([hbuf[blk, yy, zz].astype(F32) for zz in range(SIDE)], axis=0)
            for i in range(chunk // 128):
                part = hv[:, 128 * i : 128 * i + 128]
                sq = sq + part * part
            start = pl.multiple_of(yy * chunk, chunk)
            hg = (hv * gain_ref[:, pl.ds(start, chunk)]).astype(BF16)
            term = jnp.dot(hg, w_all[pl.ds(start, chunk), :], preferred_element_type=F32)
            if off == NEAR[0]:
                acc[...] = term
            else:
                acc[...] += term
        r = lax.rsqrt(jnp.sum(sq, axis=1, keepdims=True) * (1.0 / width) + epsilon)

        bcf = (acc[:, 0:n2] * r).astype(BF16)
        cb_out[2, here, :] = bcf
        bcv = silu(pre_bc[here, :] + bcf.astype(F32) * cbw_ref[3:4, :])
        b_in = bcv[:, 0:n_state]
        c_out = bcv[:, n_state:n2]
        b_buf[here, :] = b_in
        bd = jnp.sum(b_in * c_out, axis=1, keepdims=True)

        for g in range(block // group):
            c16 = c_out[group * g : group * g + group]
            base = blk * block + group * g
            total = None
            for i in range(0, group, 2):
                lhs = jnp.concatenate(
                    [jnp.where(row == i, c16, 0.0), jnp.where(row == i + 1, c16, 0.0)], axis=1
                ).astype(BF16)
                rhs = jnp.concatenate([st[base + i], st[base + i + 1]], axis=1)
                term = lax.dot_general(
                    lhs, rhs, (((1,), (1,)), ((), ())), preferred_element_type=F32
                )
                total = term if total is None else total + term
            q_buf[group * g : group * g + group, 0:hp] = total

        step = softplus(acc[:, dt0 : dt0 + 128] * r + dtb)
        decay = jnp.exp(step * neg_a)

        def each(v):
            return [jnp.broadcast_to(v[:, h : h + 1], (block, 128)) for h in range(heads)]

        steps, decays = each(step), each(decay)
        for h in range(heads):
            dec[h, here, :] = decays[h]

        def spread(v, k):
            return jnp.where(low, v[2 * k], v[min(2 * k + 1, heads - 1)])

        sq = jnp.zeros((block, 128), F32)
        for k in range(pairs):
            a = acc[:, n2 + 256 * k : n2 + 256 * k + 128]
            if 2 * k + 1 < heads:
                b = acc[:, n2 + 256 * k + 128 : n2 + 256 * k + 256]
            else:
                b = jnp.zeros_like(a)
            x_new = jnp.where(low, pltpu.roll(a, p_size, 1), b)
            z_new = jnp.where(low, a, pltpu.roll(b, p_size, 1))
            xf = (x_new * r).astype(BF16)
            xf_buf[k, here, :] = xf
            xc = silu(pre_x[k, here, :] + xf.astype(F32) * par[0, k])
            sx = spread(steps, k) * xc
            stx[k, here, :] = sx
            q = q_buf[:, 128 * k : 128 * k + 128]
            y_out = spread(decays, k) * q + sx * bd + par[2, k] * xc
            gated = y_out * silu(z_new * r)
            sq = sq + gated * gated
            inner[:, 128 * k : 128 * k + 128] = (gated * par[1, k]).astype(BF16)
        squares = jnp.sum(sq, axis=1, keepdims=True)
        hi = squares.astype(BF16).astype(F32)
        lo = squares - hi
        sq_tile = jnp.where(lane == 0, hi, jnp.where(lane == 1, lo, 0.0))

        for yo in FAR:
            yy = (jnp.where(sec < last, my_y, my_z) + yo) % SIDE
            part = jnp.dot(inner[:, 0:hp], w_o[yy], preferred_element_type=F32)

            @pl.when(sec < last)
            def _():
                whole = jnp.concatenate([part, sq_tile], axis=1)
                for zz in range(SIDE):
                    send_buf[blk, yy, zz] = whole[rows * zz : rows * zz + rows].astype(BF16)
                for zo in FAR:
                    zz = (my_z + zo) % SIDE
                    if yo == 0 and zo == 0:
                        rs_own(blk).start()
                    else:
                        rs_copy(blk, me, zz * SIDE + yy, yy, zz).start()

            @pl.when(sec == last)
            def _():
                for j in range(SIDE):
                    send_end[blk, yy, j] = jnp.concatenate(
                        [part[:, 128 * j : 128 * j + 256], sq_tile], axis=1
                    ).astype(BF16)
                for jo in FAR:
                    j = (my_y + jo) % SIDE
                    if yo == 0 and jo == 0:
                        end_own(blk).start()
                    else:
                        end_copy(blk, me, yy, j).start()

        return carry

    lax.fori_loop(0, BLOCKS, layer, 0)

    octet = 8
    per_block = block // octet

    def turn():
        zeros = jnp.zeros((128 - streams, 128), F32)
        for k in range(pairs):
            turned = jnp.concatenate([stx[k], zeros], axis=0).T
            stx_t[128 * k : 128 * k + 128] = turned[:, 0:streams].astype(BF16)

    at_stream = lax.broadcasted_iota(jnp.int32, (streams, n_state), 0)

    def update(g, carry):
        span8 = pl.ds(pl.multiple_of(g * octet, octet), octet)
        b8 = b_buf[span8, :]
        for i in range(0, octet, 2):
            rhs = jnp.concatenate(
                [jnp.where(at_stream == g * octet + i + e, b8[i + e : i + e + 1], 0.0) for e in (0, 1)],
                axis=1,
            ).astype(BF16)
            more = jnp.dot(stx_t[0:hp, :], rhs, preferred_element_type=F32)
            for e in (0, 1):
                for h in range(heads):
                    span = slice(p_size * h, p_size * h + p_size)
                    old = st[g * octet + i + e, span, :].astype(F32)
                    new = (
                        dec[h, span8, :][i + e : i + e + 1] * old
                        + more[span, n_state * e : n_state * e + n_state]
                    )
                    st[g * octet + i + e, span, :] = new.astype(BF16)
        return carry

    def sh_copy(blk, src_z, j):
        return pltpu.make_async_remote_copy(
            src_ref=ag_src.at[blk],
            dst_ref=sh_buf.at[blk, src_z],
            send_sem=sh_send.at[blk, j],
            recv_sem=sh_recv.at[blk, src_z],
            device_id=dev(sec, my_y * SIDE + j),
            device_id_type=MESH,
        )

    turn()
    for blk in range(BLOCKS):
        lax.fori_loop(EARLY[blk - 1] if blk else 0, EARLY[blk], update, 0)

        @pl.when(sec < last)
        def _():
            tot = jnp.zeros((rows, chunk + 128), F32)
            for yo in NEAR:
                for zo in NEAR:
                    src = ((my_z + zo) % SIDE) * SIDE + (my_y + yo) % SIDE
                    if yo == 0 and zo == 0:
                        rs_own(blk).wait()
                    else:
                        rs_copy(blk, src, me, my_y, my_z).wait_recv()
                    tot = tot + rs_buf[blk, src].astype(F32)
            scale = lax.rsqrt(
                jnp.sum(tot[:, chunk : chunk + 128], axis=1, keepdims=True) * (1.0 / (hp * team))
                + epsilon
            )
            mine = hbuf[blk, my_y, my_z].astype(F32)
            ag_src[blk] = (mine + tot[:, 0:chunk] * scale).astype(BF16)

            for other in ring:
                ag_copy(blk, me, other).start()

        @pl.when(sec == last)
        def _():
            tot = jnp.zeros((block, 384), F32)
            for yo in NEAR:
                for zo in NEAR:
                    src = ((my_z + zo) % SIDE) * SIDE + (my_y + yo) % SIDE
                    if yo == 0 and zo == 0:
                        end_own(blk).wait()
                    else:
                        end_copy(blk, src, my_z, my_y).wait_recv()
                    tot = tot + sum_end[blk, src].astype(F32)
            scale = lax.rsqrt(
                jnp.sum(tot[:, 256:384], axis=1, keepdims=True) * (1.0 / (hp * team)) + epsilon
            )
            window = pl.ds(pl.multiple_of(my_y * 128, 128), 256)
            mine = jnp.concatenate(
                [hbuf[blk, my_z, zz, :, window].astype(F32) for zz in range(SIDE)], axis=0
            )
            end_buf[...] = mine + tot[:, 0:256] * scale
            for j in range(SIDE):

                @pl.when(my_y == j)
                def _():
                    first = (share - 128) * j
                    sec_out[blk * block : blk * block + block, :] = end_buf[...][
                        :, first : first + share
                    ].astype(BF16)

    @pl.when(sec < last)
    def _():
        for blk in range(BLOCKS):
            for j in range(SIDE):
                own = my_y * SIDE + j == me

                @pl.when(own)
                def _():
                    pltpu.make_async_copy(
                        ag_src.at[blk], sh_buf.at[blk, my_z], sh_recv.at[blk, my_z]
                    ).start()

                @pl.when(jnp.logical_not(own))
                def _():
                    sh_copy(blk, my_z, j).start()

    lax.fori_loop(EARLY[-1], streams // octet, update, 0)

    for h in range(heads):
        xf = xf_buf[h // 2].astype(F32)
        cx_out[2, h] = xf[:, p_size * (h % 2) : p_size * (h % 2) + p_size].astype(BF16)

    @pl.when(sec < last)
    def _():
        for blk in range(BLOCKS):
            for zz in range(SIDE):
                sh_copy(blk, zz, 0).wait_recv()
        for yy in range(SIDE):

            @pl.when(my_y == yy)
            def _():
                whole = jnp.concatenate(
                    [
                        sh_buf[blk, zz].astype(F32)
                        for blk in range(BLOCKS)
                        for zz in range(SIDE)
                    ],
                    axis=0,
                )
                sec_out[...] = whole[:, share * yy : share * yy + share].astype(BF16)

    @pl.when(sec < last)
    def _():
        for blk in range(BLOCKS):
            for other in ring[:-1]:
                rs_copy(blk, me, other, my_y, my_z).wait_send()
            for dest in range(team):
                ag_copy(blk, me, dest).wait_send()
            for j in range(SIDE):

                @pl.when(my_y * SIDE + j != me)
                def _():
                    sh_copy(blk, my_z, j).wait_send()

    @pl.when(sec == last)
    def _():
        for blk in range(BLOCKS):
            for other in ring[:-1]:
                end_copy(blk, me, other // SIDE, other % SIDE).wait_send()

    @pl.when(sec == 0)
    def _():
        for blk in range(BLOCKS):
            for other in ring[:-1]:
                init_copy(blk, me, other).wait_send()


def write_out(a_in, b_in, c_in, d_in, a_out, b_out, c_out, d_out, sems):
    size = d_in.shape[0] // PIECES
    copies = [
        pltpu.make_async_copy(d_in.at[pl.ds(size * i, size)], d_out.at[pl.ds(size * i, size)], sems.at[3 + i])
        for i in range(PIECES)
    ]
    for i, (x, y) in enumerate(((a_in, a_out), (b_in, b_out), (c_in, c_out))):
        copies.append(pltpu.make_async_copy(x, y, sems.at[i]))
    for cp in copies:
        cp.start()
    for cp in copies:
        cp.wait()


def shards(
    hidden_in,
    pre_gain,
    w_zx,
    w_bc,
    w_dt,
    dt_bias,
    a_log,
    d_skip,
    conv_x_weight,
    conv_x_bias,
    conv_bc_weight,
    conv_bc_bias,
    inner_gain,
    w_out,
    conv_x_state,
    conv_bc_state,
    ssm_state,
    sections,
):
    streams, share = hidden_in.shape
    _, heads, p_size, width = w_out.shape
    n2 = w_bc.shape[2]
    n_state = n2 // 2
    team = SIDE * SIDE
    chunk, block = width // SIDE, streams // BLOCKS
    rows = block // SIDE
    hp = heads * p_size
    cols = n2 + 128 * heads + 128
    pairs = (heads + 1) // 2
    args = (
        hidden_in,
        pre_gain,
        jnp.transpose(w_zx[0], (1, 0, 2)),
        w_bc[0],
        jnp.transpose(w_dt[0], (1, 0)),
        dt_bias,
        a_log,
        d_skip,
        jnp.transpose(conv_x_weight[0], (1, 0, 2)),
        jnp.transpose(conv_x_bias, (1, 0, 2)),
        conv_bc_weight[0],
        conv_bc_bias,
        jnp.transpose(inner_gain, (1, 0, 2)),
        w_out[0].reshape(hp, width),
        jnp.transpose(conv_x_state[0], (1, 2, 0, 3)),
        jnp.transpose(conv_bc_state[0], (1, 0, 2)),
        ssm_state[0].reshape(streams, hp, n_state),
    )
    vmem = pl.BlockSpec(memory_space=pltpu.VMEM)
    hbm = pl.BlockSpec(memory_space=pltpu.HBM)
    small = (1, 4, 5, 6, 7, 8, 9, 10, 11, 12, 14, 15)
    dma = pltpu.SemaphoreType.DMA
    sec_new, cx_new, cb_new, ssm_new = pl.pallas_call(
        functools.partial(kernel, sections),
        out_shape=(
            jax.ShapeDtypeStruct((streams, share), BF16),
            jax.ShapeDtypeStruct((3, heads, streams, p_size), BF16),
            jax.ShapeDtypeStruct((3, streams, n2), BF16),
            jax.ShapeDtypeStruct((streams, hp, n_state), BF16),
        ),
        in_specs=[hbm] * len(args),
        out_specs=(vmem, vmem, vmem, vmem),
        scratch_shapes=[
            pltpu.VMEM((streams, share), BF16),
            pltpu.VMEM((BLOCKS, rows, chunk), BF16),
        ]
        + [pltpu.VMEM(args[i].shape, args[i].dtype) for i in small]
        + [
            pltpu.VMEM((width, cols), BF16),
            pltpu.VMEM((SIDE, hp, chunk), BF16),
            pltpu.VMEM((BLOCKS, SIDE, SIDE, rows, chunk), BF16),
            pltpu.VMEM((block, cols), F32),
            pltpu.VMEM((128, width), F32),
            pltpu.VMEM((streams, n2), F32),
            pltpu.VMEM((pairs, streams, 128), F32),
            pltpu.VMEM((3, pairs, 1, 128), F32),
            pltpu.VMEM((block, 128 * pairs), F32),
            pltpu.VMEM((block, 128 * pairs), BF16),
            pltpu.VMEM((pairs, streams, 128), F32),
            pltpu.VMEM((heads, streams, 128), F32),
            pltpu.VMEM((streams, n_state), F32),
            pltpu.VMEM((pairs, streams, 128), BF16),
            pltpu.VMEM((128 * pairs, streams), BF16),
            pltpu.VMEM((BLOCKS, SIDE, SIDE, rows, chunk + 128), BF16),
            pltpu.VMEM((BLOCKS, team, rows, chunk + 128), BF16),
            pltpu.VMEM((BLOCKS, rows, chunk), BF16),
            pltpu.VMEM((BLOCKS, team, rows, chunk), BF16),
            pltpu.VMEM((BLOCKS, SIDE, rows, chunk), BF16),
            pltpu.VMEM((BLOCKS, SIDE, SIDE, block, 384), BF16),
            pltpu.VMEM((BLOCKS, team, block, 384), BF16),
            pltpu.VMEM((block, 256), F32),
            dma(()),
            dma((1 + heads + SIDE + 1,)),
            dma((len(small),)),
            dma((BLOCKS, team)),
            dma((BLOCKS, team)),
            dma((BLOCKS, team)),
            dma((BLOCKS, team)),
            dma((BLOCKS, team)),
            dma((BLOCKS, team)),
            dma((BLOCKS, SIDE)),
            dma((BLOCKS, SIDE)),
        ],
        compiler_params=pltpu.CompilerParams(
            collective_id=0, has_side_effects=True, vmem_limit_bytes=40 * 1024 * 1024
        ),
        name="stack_step",
    )(*[pltpu.with_memory_space_constraint(a, pltpu.HBM) for a in args])
    results = (sec_new, cx_new, cb_new, ssm_new)
    sec_new, cx_new, cb_new, ssm_new = pl.pallas_call(
        write_out,
        out_shape=tuple(jax.ShapeDtypeStruct(a.shape, a.dtype) for a in results),
        in_specs=[vmem] * 4,
        out_specs=(pl.BlockSpec(memory_space=pltpu.HBM),) * 4,
        scratch_shapes=[dma((3 + PIECES,))],
        compiler_params=pltpu.CompilerParams(vmem_limit_bytes=16 * 1024 * 1024),
        name="write_out",
    )(*results)
    return (
        sec_new[None],
        jnp.transpose(cx_new, (2, 0, 1, 3))[None],
        jnp.transpose(cb_new, (1, 0, 2))[None],
        ssm_new.reshape(ssm_state.shape),
    )


def solution(mesh):
    placed = (
        P(None, "tensor"),
        P("section", None),
        P("section", None, "tensor", None),
        P("section", None, None),
        P("section", None, "tensor"),
        P("section", "tensor"),
        P("section", "tensor"),
        P("section", "tensor"),
        P("section", None, "tensor", None),
        P("section", "tensor", None),
        P("section", None, None),
        P("section", None),
        P("section", "tensor", None),
        P("section", "tensor", None, None),
        P("section", None, None, "tensor", None),
        P("section", None, None, None),
        P("section", None, "tensor", None, None),
    )
    return jax.shard_map(
        functools.partial(shards, sections=mesh.shape["section"]),
        mesh=mesh,
        in_specs=placed,
        out_specs=(
            P("section", None, "tensor"),
            P("section", None, None, "tensor", None),
            P("section", None, None, None),
            P("section", None, "tensor", None, None),
        ),
        check_vma=False,
    )
```

```python
import functools

import jax
import jax.numpy as jnp
from jax import lax
from jax.experimental import pallas as pl
from jax.experimental.pallas import tpu as pltpu
from jax.sharding import PartitionSpec as P

epsilon = 1e-05
MESH = pl.DeviceIdType.MESH
F32, BF16 = jnp.float32, jnp.bfloat16
SIDE = 4
NEAR = (0, 1, 3, 2)
FAR = (2, 1, 3, 0)
PIECES = 4
BLOCKS = 2
EARLY = (4, 8)


def silu(v):
    return v / (1.0 + jnp.exp(-v))


def softplus(v):
    return jnp.maximum(v, 0.0) + jnp.log1p(jnp.exp(-jnp.abs(v)))


def kernel(
    sections,
    hid_hbm,
    gain_hbm,
    wzx_hbm,
    wbc_hbm,
    wdt_hbm,
    dtb_hbm,
    alog_hbm,
    dsk_hbm,
    cxw_hbm,
    cxb_hbm,
    cbw_hbm,
    cbb_hbm,
    ig_hbm,
    wout_hbm,
    cxs_hbm,
    cbs_hbm,
    ssm_hbm,
    sec_out,
    cx_out,
    cb_out,
    st,
    hid_ref,
    pack,
    gain_ref,
    wdt_ref,
    dtb_ref,
    alog_ref,
    dsk_ref,
    cxw_ref,
    cxb_ref,
    cbw_ref,
    cbb_ref,
    ig_ref,
    cxs_ref,
    cbs_ref,
    w_all,
    w_o,
    hbuf,
    acc,
    wdt_pad,
    pre_bc,
    pre_x,
    par,
    q_buf,
    inner,
    stx,
    dec,
    b_buf,
    xf_buf,
    stx_t,
    send_buf,
    rs_buf,
    ag_src,
    init_buf,
    sh_buf,
    send_end,
    sum_end,
    end_buf,
    hid_sem,
    load_sem,
    small_sem,
    init_send,
    init_recv,
    rs_send,
    rs_recv,
    ag_send,
    ag_recv,
    sh_send,
    sh_recv,
):
    heads, streams, p_size = cxs_hbm.shape[1:]
    width, n2 = wbc_hbm.shape
    n_state = n2 // 2
    chunk = width // SIDE
    block = streams // BLOCKS
    rows = block // SIDE
    share = hid_hbm.shape[1]
    team = SIDE * SIDE
    last = sections - 1

    sec = lax.axis_index("section")
    me = lax.axis_index("tensor")
    my_z = me // SIDE
    my_y = me % SIDE

    def dev(s, t):
        return {"section": s, "tensor": t}

    loads = [pltpu.make_async_copy(wbc_hbm, w_all.at[:, pl.ds(0, n2)], load_sem.at[0])]
    for h in range(heads):
        loads.append(
            pltpu.make_async_copy(
                wzx_hbm.at[h], w_all.at[:, pl.ds(n2 + 128 * h, 128)], load_sem.at[1 + h]
            )
        )
    at = 1 + heads
    for yy in range(SIDE):
        loads.append(
            pltpu.make_async_copy(
                wout_hbm.at[:, pl.ds(chunk * yy, chunk)], w_o.at[yy], load_sem.at[at + yy]
            )
        )
    at += SIDE
    loads.append(pltpu.make_async_copy(ssm_hbm, st, load_sem.at[at]))
    smalls = [
        pltpu.make_async_copy(a, b, small_sem.at[i])
        for i, (a, b) in enumerate(
            (
                (wdt_hbm, wdt_ref),
                (gain_hbm, gain_ref),
                (dtb_hbm, dtb_ref),
                (alog_hbm, alog_ref),
                (dsk_hbm, dsk_ref),
                (cxw_hbm, cxw_ref),
                (cxb_hbm, cxb_ref),
                (cbw_hbm, cbw_ref),
                (cbb_hbm, cbb_ref),
                (ig_hbm, ig_ref),
                (cxs_hbm, cxs_ref),
                (cbs_hbm, cbs_ref),
            )
        )
    ]

    barrier = pltpu.get_barrier_semaphore()

    ring = [
        ((my_z + zo) % SIDE) * SIDE + (my_y + yo) % SIDE
        for yo, zo in sorted(
            ((yo, zo) for yo in FAR for zo in FAR),
            key=lambda o: sum(min(v, SIDE - v) for v in o),
            reverse=True,
        )
    ]

    for other in ring[:-1]:
        pl.semaphore_signal(barrier, inc=1, device_id=dev(sec, other), device_id_type=MESH)

    @pl.when(sec > 0)
    def _():
        for other in ring:
            pl.semaphore_signal(barrier, inc=1, device_id=dev(sec - 1, other), device_id_type=MESH)

    @pl.when(sec < last)
    def _():
        for other in ring:
            pl.semaphore_signal(barrier, inc=1, device_id=dev(sec + 1, other), device_id_type=MESH)

    hid_copy = pltpu.make_async_copy(hid_hbm, hid_ref, hid_sem)
    hid_copy.start()
    for cp in smalls + loads:
        cp.start()

    hid_copy.wait()
    for blk in range(BLOCKS):
        parts = [
            hid_ref[blk * block + rows * zz : blk * block + rows * zz + rows, :].astype(F32)
            if rows % 16 == 0
            else hid_ref[blk * block : blk * block + block, :].astype(F32)[rows * zz : rows * zz + rows]
            for zz in range(SIDE)
        ]
        pack[blk] = jnp.concatenate(parts, axis=1).astype(BF16)

    partners = team - 1 + jnp.where(sec > 0, team, 0) + jnp.where(sec < last, team, 0)
    pl.semaphore_wait(barrier, partners)

    def init_copy(blk, src_t, dest):
        return pltpu.make_async_remote_copy(
            src_ref=pack.at[blk],
            dst_ref=init_buf.at[blk, src_t],
            send_sem=init_send.at[blk, dest],
            recv_sem=init_recv.at[blk, src_t],
            device_id=dev(sec, dest),
            device_id_type=MESH,
        )

    def init_own(blk):
        return pltpu.make_async_copy(
            pack.at[blk], init_buf.at[blk, me], init_recv.at[blk, me]
        )

    @pl.when(sec == 0)
    def _():
        for blk in range(BLOCKS):
            for other in ring[:-1]:
                init_copy(blk, me, other).start()
            init_own(blk).start()

    for cp in smalls:
        cp.wait()
    wdt_pad[...] = jnp.zeros_like(wdt_pad)
    wdt_pad[0:heads, :] = wdt_ref[...].astype(F32)
    for h in range(1 + heads):
        loads[h].wait()
    for j in range(width // 128):
        blk = wdt_pad[:, 128 * j : 128 * j + 128]
        w_all[128 * j : 128 * j + 128, n2 + 128 * heads : n2 + 128 * heads + 128] = blk.T.astype(BF16)
    q_buf[...] = jnp.zeros_like(q_buf)
    cb_out[0] = cbs_ref[1]
    cb_out[1] = cbs_ref[2]
    cx_out[0] = cxs_ref[1]
    cx_out[1] = cxs_ref[2]
    cbw = cbw_ref[...]
    pre_bc[...] = (
        cbs_ref[0].astype(F32) * cbw[0:1]
        + cbs_ref[1].astype(F32) * cbw[1:2]
        + cbs_ref[2].astype(F32) * cbw[2:3]
        + cbb_ref[...]
    )
    pairs = (heads + 1) // 2

    def packed(get, k):
        a = get(2 * k)
        b = get(2 * k + 1) if 2 * k + 1 < heads else jnp.zeros_like(a)
        return jnp.concatenate([a, b], axis=1)

    def pre_of(h):
        w = cxw_ref[h]
        return (
            cxs_ref[0, h].astype(F32) * w[0:1]
            + cxs_ref[1, h].astype(F32) * w[1:2]
            + cxs_ref[2, h].astype(F32) * w[2:3]
            + cxb_ref[h]
        )

    for k in range(pairs):
        pre_x[k] = packed(pre_of, k)
        par[0, k] = packed(lambda h: cxw_ref[h][3:4], k)
        par[1, k] = packed(lambda h: ig_ref[h], k)
        par[2, k] = packed(
            lambda h: jnp.broadcast_to(dsk_ref[:, h : h + 1], (1, p_size)), k
        )
    pad = jnp.zeros((1, 128 - heads), F32)
    dtb = jnp.concatenate([dtb_ref[...], pad], axis=1)
    neg_a = -jnp.exp(jnp.concatenate([alog_ref[...], pad], axis=1))

    def ag_copy(blk, src_t, dest):
        return pltpu.make_async_remote_copy(
            src_ref=ag_src.at[blk],
            dst_ref=hbuf.at[blk, src_t % SIDE, src_t // SIDE],
            send_sem=ag_send.at[blk, dest],
            recv_sem=ag_recv.at[blk, src_t],
            device_id=dev(jnp.minimum(sec + 1, last), dest),
            device_id_type=MESH,
        )

    def rs_copy(blk, src_t, dest, yy, zz):
        return pltpu.make_async_remote_copy(
            src_ref=send_buf.at[blk, yy, zz],
            dst_ref=rs_buf.at[blk, src_t],
            send_sem=rs_send.at[blk, dest],
            recv_sem=rs_recv.at[blk, src_t],
            device_id=dev(sec, dest),
            device_id_type=MESH,
        )

    def rs_own(blk):
        return pltpu.make_async_copy(
            send_buf.at[blk, my_y, my_z], rs_buf.at[blk, me], rs_recv.at[blk, me]
        )

    def end_copy(blk, src_t, zz, j):
        return pltpu.make_async_remote_copy(
            src_ref=send_end.at[blk, zz, j],
            dst_ref=sum_end.at[blk, src_t],
            send_sem=rs_send.at[blk, zz * SIDE + j],
            recv_sem=rs_recv.at[blk, src_t],
            device_id=dev(sec, zz * SIDE + j),
            device_id_type=MESH,
        )

    def end_own(blk):
        return pltpu.make_async_copy(
            send_end.at[blk, my_z, my_y], sum_end.at[blk, me], rs_recv.at[blk, me]
        )

    for cp in loads[1 + heads :]:
        cp.wait()
    lane = lax.broadcasted_iota(jnp.int32, (block, 128), 1)
    low = lane < p_size
    hp = heads * p_size
    dt0 = n2 + 128 * heads
    group = 16
    row = lax.broadcasted_iota(jnp.int32, (group, n_state), 0)

    def layer(blk, carry):
        here = pl.ds(pl.multiple_of(blk * block, block), block)

        @pl.when(sec == 0)
        def _():
            for other in ring[:-1]:
                init_copy(blk, other, me).wait_recv()
            init_own(blk).wait()
            for yy in range(SIDE):
                parts = [init_buf[blk, SIDE * yy + i].astype(F32) for i in range(SIDE)]
                for zz in range(SIDE):
                    hbuf[blk, yy, zz] = jnp.concatenate(
                        [part[:, share * zz : share * zz + share] for part in parts], axis=1
                    ).astype(BF16)

        sq = jnp.zeros((block, 128), F32)
        for off in NEAR:
            yy = (my_y + off) % SIDE

            @pl.when(sec > 0)
            def _():
                for zo in NEAR:
                    ag_copy(blk, ((my_z + zo) % SIDE) * SIDE + yy, me).wait_recv()

            hv = jnp.concatenate([hbuf[blk, yy, zz].astype(F32) for zz in range(SIDE)], axis=0)
            for i in range(chunk // 128):
                part = hv[:, 128 * i : 128 * i + 128]
                sq = sq + part * part
            start = pl.multiple_of(yy * chunk, chunk)
            hg = (hv * gain_ref[:, pl.ds(start, chunk)]).astype(BF16)
            term = jnp.dot(hg, w_all[pl.ds(start, chunk), :], preferred_element_type=F32)
            if off == NEAR[0]:
                acc[...] = term
            else:
                acc[...] += term
        r = lax.rsqrt(jnp.sum(sq, axis=1, keepdims=True) * (1.0 / width) + epsilon)

        bcf = (acc[:, 0:n2] * r).astype(BF16)
        cb_out[2, here, :] = bcf
        bcv = silu(pre_bc[here, :] + bcf.astype(F32) * cbw_ref[3:4, :])
        b_in = bcv[:, 0:n_state]
        c_out = bcv[:, n_state:n2]
        b_buf[here, :] = b_in
        bd = jnp.sum(b_in * c_out, axis=1, keepdims=True)

        for g in range(block // group):
            c16 = c_out[group * g : group * g + group]
            base = blk * block + group * g
            total = None
            for i in range(0, group, 2):
                lhs = jnp.concatenate(
                    [jnp.where(row == i, c16, 0.0), jnp.where(row == i + 1, c16, 0.0)], axis=1
                ).astype(BF16)
                rhs = jnp.concatenate([st[base + i], st[base + i + 1]], axis=1)
                term = lax.dot_general(
                    lhs, rhs, (((1,), (1,)), ((), ())), preferred_element_type=F32
                )
                total = term if total is None else total + term
            q_buf[group * g : group * g + group, 0:hp] = total

        step = softplus(acc[:, dt0 : dt0 + 128] * r + dtb)
        decay = jnp.exp(step * neg_a)

        def each(v):
            return [jnp.broadcast_to(v[:, h : h + 1], (block, 128)) for h in range(heads)]

        steps, decays = each(step), each(decay)
        for h in range(heads):
            dec[h, here, :] = decays[h]

        def spread(v, k):
            return jnp.where(low, v[2 * k], v[min(2 * k + 1, heads - 1)])

        sq = jnp.zeros((block, 128), F32)
        for k in range(pairs):
            a = acc[:, n2 + 256 * k : n2 + 256 * k + 128]
            if 2 * k + 1 < heads:
                b = acc[:, n2 + 256 * k + 128 : n2 + 256 * k + 256]
            else:
                b = jnp.zeros_like(a)
            x_new = jnp.where(low, pltpu.roll(a, p_size, 1), b)
            z_new = jnp.where(low, a, pltpu.roll(b, p_size, 1))
            xf = (x_new * r).astype(BF16)
            xf_buf[k, here, :] = xf
            xc = silu(pre_x[k, here, :] + xf.astype(F32) * par[0, k])
            sx = spread(steps, k) * xc
            stx[k, here, :] = sx
            q = q_buf[:, 128 * k : 128 * k + 128]
            y_out = spread(decays, k) * q + sx * bd + par[2, k] * xc
            gated = y_out * silu(z_new * r)
            sq = sq + gated * gated
            inner[:, 128 * k : 128 * k + 128] = (gated * par[1, k]).astype(BF16)
        squares = jnp.sum(sq, axis=1, keepdims=True)
        hi = squares.astype(BF16).astype(F32)
        lo = squares - hi
        sq_tile = jnp.where(lane == 0, hi, jnp.where(lane == 1, lo, 0.0))

        for yo in FAR:
            yy = (jnp.where(sec < last, my_y, my_z) + yo) % SIDE
            part = jnp.dot(inner[:, 0:hp], w_o[yy], preferred_element_type=F32)

            @pl.when(sec < last)
            def _():
                whole = jnp.concatenate([part, sq_tile], axis=1)
                for zz in range(SIDE):
                    send_buf[blk, yy, zz] = whole[rows * zz : rows * zz + rows].astype(BF16)
                for zo in FAR:
                    zz = (my_z + zo) % SIDE
                    if yo == 0 and zo == 0:
                        rs_own(blk).start()
                    else:
                        rs_copy(blk, me, zz * SIDE + yy, yy, zz).start()

            @pl.when(sec == last)
            def _():
                for j in range(SIDE):
                    send_end[blk, yy, j] = jnp.concatenate(
                        [part[:, 128 * j : 128 * j + 256], sq_tile], axis=1
                    ).astype(BF16)
                for jo in FAR:
                    j = (my_y + jo) % SIDE
                    if yo == 0 and jo == 0:
                        end_own(blk).start()
                    else:
                        end_copy(blk, me, yy, j).start()

        return carry

    lax.fori_loop(0, BLOCKS, layer, 0)

    octet = 8
    per_block = block // octet

    def turn():
        zeros = jnp.zeros((128 - streams, 128), F32)
        for k in range(pairs):
            turned = jnp.concatenate([stx[k], zeros], axis=0).T
            stx_t[128 * k : 128 * k + 128] = turned[:, 0:streams].astype(BF16)

    at_stream = lax.broadcasted_iota(jnp.int32, (streams, n_state), 0)

    def update(g, carry):
        span8 = pl.ds(pl.multiple_of(g * octet, octet), octet)
        b8 = b_buf[span8, :]
        for i in range(0, octet, 2):
            rhs = jnp.concatenate(
                [jnp.where(at_stream == g * octet + i + e, b8[i + e : i + e + 1], 0.0) for e in (0, 1)],
                axis=1,
            ).astype(BF16)
            more = jnp.dot(stx_t[0:hp, :], rhs, preferred_element_type=F32)
            for e in (0, 1):
                for h in range(heads):
                    span = slice(p_size * h, p_size * h + p_size)
                    old = st[g * octet + i + e, span, :].astype(F32)
                    new = (
                        dec[h, span8, :][i + e : i + e + 1] * old
                        + more[span, n_state * e : n_state * e + n_state]
                    )
                    st[g * octet + i + e, span, :] = new.astype(BF16)
        return carry

    def sh_copy(blk, src_z, j):
        return pltpu.make_async_remote_copy(
            src_ref=ag_src.at[blk],
            dst_ref=sh_buf.at[blk, src_z],
            send_sem=sh_send.at[blk, j],
            recv_sem=sh_recv.at[blk, src_z],
            device_id=dev(sec, my_y * SIDE + j),
            device_id_type=MESH,
        )

    @pl.when(sec == last)
    def _():
        turn()

    for blk in range(BLOCKS):
        lax.fori_loop(
            EARLY[blk - 1] if blk else 0,
            jnp.where(sec == last, EARLY[blk], EARLY[blk - 1] if blk else 0),
            update,
            0,
        )

        @pl.when(sec < last)
        def _():
            tot = jnp.zeros((rows, chunk + 128), F32)
            for yo in NEAR:
                for zo in NEAR:
                    src = ((my_z + zo) % SIDE) * SIDE + (my_y + yo) % SIDE
                    if yo == 0 and zo == 0:
                        rs_own(blk).wait()
                    else:
                        rs_copy(blk, src, me, my_y, my_z).wait_recv()
                    tot = tot + rs_buf[blk, src].astype(F32)
            scale = lax.rsqrt(
                jnp.sum(tot[:, chunk : chunk + 128], axis=1, keepdims=True) * (1.0 / (hp * team))
                + epsilon
            )
            mine = hbuf[blk, my_y, my_z].astype(F32)
            ag_src[blk] = (mine + tot[:, 0:chunk] * scale).astype(BF16)

            for other in ring:
                ag_copy(blk, me, other).start()

        @pl.when(sec == last)
        def _():
            tot = jnp.zeros((block, 384), F32)
            for yo in NEAR:
                for zo in NEAR:
                    src = ((my_z + zo) % SIDE) * SIDE + (my_y + yo) % SIDE
                    if yo == 0 and zo == 0:
                        end_own(blk).wait()
                    else:
                        end_copy(blk, src, my_z, my_y).wait_recv()
                    tot = tot + sum_end[blk, src].astype(F32)
            scale = lax.rsqrt(
                jnp.sum(tot[:, 256:384], axis=1, keepdims=True) * (1.0 / (hp * team)) + epsilon
            )
            window = pl.ds(pl.multiple_of(my_y * 128, 128), 256)
            mine = jnp.concatenate(
                [hbuf[blk, my_z, zz, :, window].astype(F32) for zz in range(SIDE)], axis=0
            )
            end_buf[...] = mine + tot[:, 0:256] * scale
            for j in range(SIDE):

                @pl.when(my_y == j)
                def _():
                    first = (share - 128) * j
                    sec_out[blk * block : blk * block + block, :] = end_buf[...][
                        :, first : first + share
                    ].astype(BF16)

    @pl.when(sec < last)
    def _():
        for blk in range(BLOCKS):
            for j in range(SIDE):
                own = my_y * SIDE + j == me

                @pl.when(own)
                def _():
                    pltpu.make_async_copy(
                        ag_src.at[blk], sh_buf.at[blk, my_z], sh_recv.at[blk, my_z]
                    ).start()

                @pl.when(jnp.logical_not(own))
                def _():
                    sh_copy(blk, my_z, j).start()

    @pl.when(sec < last)
    def _():
        turn()

    lax.fori_loop(jnp.where(sec == last, EARLY[-1], 0), streams // octet, update, 0)

    for h in range(heads):
        xf = xf_buf[h // 2].astype(F32)
        cx_out[2, h] = xf[:, p_size * (h % 2) : p_size * (h % 2) + p_size].astype(BF16)

    @pl.when(sec < last)
    def _():
        for blk in range(BLOCKS):
            for zz in range(SIDE):
                sh_copy(blk, zz, 0).wait_recv()
        for yy in range(SIDE):

            @pl.when(my_y == yy)
            def _():
                whole = jnp.concatenate(
                    [
                        sh_buf[blk, zz].astype(F32)
                        for blk in range(BLOCKS)
                        for zz in range(SIDE)
                    ],
                    axis=0,
                )
                sec_out[...] = whole[:, share * yy : share * yy + share].astype(BF16)

    @pl.when(sec < last)
    def _():
        for blk in range(BLOCKS):
            for other in ring[:-1]:
                rs_copy(blk, me, other, my_y, my_z).wait_send()
            for dest in range(team):
                ag_copy(blk, me, dest).wait_send()
            for j in range(SIDE):

                @pl.when(my_y * SIDE + j != me)
                def _():
                    sh_copy(blk, my_z, j).wait_send()

    @pl.when(sec == last)
    def _():
        for blk in range(BLOCKS):
            for other in ring[:-1]:
                end_copy(blk, me, other // SIDE, other % SIDE).wait_send()

    @pl.when(sec == 0)
    def _():
        for blk in range(BLOCKS):
            for other in ring[:-1]:
                init_copy(blk, me, other).wait_send()


def write_out(a_in, b_in, c_in, d_in, a_out, b_out, c_out, d_out, sems):
    size = d_in.shape[0] // PIECES
    copies = [
        pltpu.make_async_copy(d_in.at[pl.ds(size * i, size)], d_out.at[pl.ds(size * i, size)], sems.at[3 + i])
        for i in range(PIECES)
    ]
    for i, (x, y) in enumerate(((a_in, a_out), (b_in, b_out), (c_in, c_out))):
        copies.append(pltpu.make_async_copy(x, y, sems.at[i]))
    for cp in copies:
        cp.start()
    for cp in copies:
        cp.wait()


def shards(
    hidden_in,
    pre_gain,
    w_zx,
    w_bc,
    w_dt,
    dt_bias,
    a_log,
    d_skip,
    conv_x_weight,
    conv_x_bias,
    conv_bc_weight,
    conv_bc_bias,
    inner_gain,
    w_out,
    conv_x_state,
    conv_bc_state,
    ssm_state,
    sections,
):
    streams, share = hidden_in.shape
    _, heads, p_size, width = w_out.shape
    n2 = w_bc.shape[2]
    n_state = n2 // 2
    team = SIDE * SIDE
    chunk, block = width // SIDE, streams // BLOCKS
    rows = block // SIDE
    hp = heads * p_size
    cols = n2 + 128 * heads + 128
    pairs = (heads + 1) // 2
    args = (
        hidden_in,
        pre_gain,
        jnp.transpose(w_zx[0], (1, 0, 2)),
        w_bc[0],
        jnp.transpose(w_dt[0], (1, 0)),
        dt_bias,
        a_log,
        d_skip,
        jnp.transpose(conv_x_weight[0], (1, 0, 2)),
        jnp.transpose(conv_x_bias, (1, 0, 2)),
        conv_bc_weight[0],
        conv_bc_bias,
        jnp.transpose(inner_gain, (1, 0, 2)),
        w_out[0].reshape(hp, width),
        jnp.transpose(conv_x_state[0], (1, 2, 0, 3)),
        jnp.transpose(conv_bc_state[0], (1, 0, 2)),
        ssm_state[0].reshape(streams, hp, n_state),
    )
    vmem = pl.BlockSpec(memory_space=pltpu.VMEM)
    hbm = pl.BlockSpec(memory_space=pltpu.HBM)
    small = (1, 4, 5, 6, 7, 8, 9, 10, 11, 12, 14, 15)
    dma = pltpu.SemaphoreType.DMA
    sec_new, cx_new, cb_new, ssm_new = pl.pallas_call(
        functools.partial(kernel, sections),
        out_shape=(
            jax.ShapeDtypeStruct((streams, share), BF16),
            jax.ShapeDtypeStruct((3, heads, streams, p_size), BF16),
            jax.ShapeDtypeStruct((3, streams, n2), BF16),
            jax.ShapeDtypeStruct((streams, hp, n_state), BF16),
        ),
        in_specs=[hbm] * len(args),
        out_specs=(vmem, vmem, vmem, vmem),
        scratch_shapes=[
            pltpu.VMEM((streams, share), BF16),
            pltpu.VMEM((BLOCKS, rows, chunk), BF16),
        ]
        + [pltpu.VMEM(args[i].shape, args[i].dtype) for i in small]
        + [
            pltpu.VMEM((width, cols), BF16),
            pltpu.VMEM((SIDE, hp, chunk), BF16),
            pltpu.VMEM((BLOCKS, SIDE, SIDE, rows, chunk), BF16),
            pltpu.VMEM((block, cols), F32),
            pltpu.VMEM((128, width), F32),
            pltpu.VMEM((streams, n2), F32),
            pltpu.VMEM((pairs, streams, 128), F32),
            pltpu.VMEM((3, pairs, 1, 128), F32),
            pltpu.VMEM((block, 128 * pairs), F32),
            pltpu.VMEM((block, 128 * pairs), BF16),
            pltpu.VMEM((pairs, streams, 128), F32),
            pltpu.VMEM((heads, streams, 128), F32),
            pltpu.VMEM((streams, n_state), F32),
            pltpu.VMEM((pairs, streams, 128), BF16),
            pltpu.VMEM((128 * pairs, streams), BF16),
            pltpu.VMEM((BLOCKS, SIDE, SIDE, rows, chunk + 128), BF16),
            pltpu.VMEM((BLOCKS, team, rows, chunk + 128), BF16),
            pltpu.VMEM((BLOCKS, rows, chunk), BF16),
            pltpu.VMEM((BLOCKS, team, rows, chunk), BF16),
            pltpu.VMEM((BLOCKS, SIDE, rows, chunk), BF16),
            pltpu.VMEM((BLOCKS, SIDE, SIDE, block, 384), BF16),
            pltpu.VMEM((BLOCKS, team, block, 384), BF16),
            pltpu.VMEM((block, 256), F32),
            dma(()),
            dma((1 + heads + SIDE + 1,)),
            dma((len(small),)),
            dma((BLOCKS, team)),
            dma((BLOCKS, team)),
            dma((BLOCKS, team)),
            dma((BLOCKS, team)),
            dma((BLOCKS, team)),
            dma((BLOCKS, team)),
            dma((BLOCKS, SIDE)),
            dma((BLOCKS, SIDE)),
        ],
        compiler_params=pltpu.CompilerParams(
            collective_id=0, has_side_effects=True, vmem_limit_bytes=40 * 1024 * 1024
        ),
        name="stack_step",
    )(*[pltpu.with_memory_space_constraint(a, pltpu.HBM) for a in args])
    results = (sec_new, cx_new, cb_new, ssm_new)
    sec_new, cx_new, cb_new, ssm_new = pl.pallas_call(
        write_out,
        out_shape=tuple(jax.ShapeDtypeStruct(a.shape, a.dtype) for a in results),
        in_specs=[vmem] * 4,
        out_specs=(pl.BlockSpec(memory_space=pltpu.HBM),) * 4,
        scratch_shapes=[dma((3 + PIECES,))],
        compiler_params=pltpu.CompilerParams(vmem_limit_bytes=16 * 1024 * 1024),
        name="write_out",
    )(*results)
    return (
        sec_new[None],
        jnp.transpose(cx_new, (2, 0, 1, 3))[None],
        jnp.transpose(cb_new, (1, 0, 2))[None],
        ssm_new.reshape(ssm_state.shape),
    )


def solution(mesh):
    placed = (
        P(None, "tensor"),
        P("section", None),
        P("section", None, "tensor", None),
        P("section", None, None),
        P("section", None, "tensor"),
        P("section", "tensor"),
        P("section", "tensor"),
        P("section", "tensor"),
        P("section", None, "tensor", None),
        P("section", "tensor", None),
        P("section", None, None),
        P("section", None),
        P("section", "tensor", None),
        P("section", "tensor", None, None),
        P("section", None, None, "tensor", None),
        P("section", None, None, None),
        P("section", None, "tensor", None, None),
    )
    return jax.shard_map(
        functools.partial(shards, sections=mesh.shape["section"]),
        mesh=mesh,
        in_specs=placed,
        out_specs=(
            P("section", None, "tensor"),
            P("section", None, None, "tensor", None),
            P("section", None, None, None),
            P("section", None, "tensor", None, None),
        ),
        check_vma=False,
    )
```

```python
import functools

import jax
import jax.numpy as jnp
from jax import lax
from jax.experimental import pallas as pl
from jax.experimental.pallas import tpu as pltpu
from jax.sharding import PartitionSpec as P

epsilon = 1e-05
MESH = pl.DeviceIdType.MESH
F32, BF16 = jnp.float32, jnp.bfloat16
SIDE = 4
NEAR = (0, 1, 3, 2)
FAR = (2, 1, 3, 0)
PIECES = 4
BLOCKS = 2
EARLY = (4, 8)


def silu(v):
    return v / (1.0 + jnp.exp(-v))


def softplus(v):
    return jnp.maximum(v, 0.0) + jnp.log1p(jnp.exp(-jnp.abs(v)))


def kernel(
    sections,
    hid_hbm,
    gain_hbm,
    wzx_hbm,
    wbc_hbm,
    wdt_hbm,
    dtb_hbm,
    alog_hbm,
    dsk_hbm,
    cxw_hbm,
    cxb_hbm,
    cbw_hbm,
    cbb_hbm,
    ig_hbm,
    wout_hbm,
    cxs_hbm,
    cbs_hbm,
    ssm_hbm,
    sec_out,
    cx_out,
    cb_out,
    st,
    hid_ref,
    pack,
    gain_ref,
    wdt_ref,
    dtb_ref,
    alog_ref,
    dsk_ref,
    cxw_ref,
    cxb_ref,
    cbw_ref,
    cbb_ref,
    ig_ref,
    cxs_ref,
    cbs_ref,
    w_all,
    w_o,
    hbuf,
    acc,
    wdt_pad,
    pre_bc,
    pre_x,
    par,
    q_buf,
    inner,
    stx,
    dec,
    b_buf,
    xf_buf,
    stx_t,
    send_buf,
    rs_buf,
    ag_src,
    init_buf,
    sh_buf,
    send_end,
    sum_end,
    end_buf,
    hid_sem,
    load_sem,
    small_sem,
    init_send,
    init_recv,
    rs_send,
    rs_recv,
    ag_send,
    ag_recv,
    sh_send,
    sh_recv,
):
    heads, streams, p_size = cxs_hbm.shape[1:]
    width, n2 = wbc_hbm.shape
    n_state = n2 // 2
    chunk = width // SIDE
    block = streams // BLOCKS
    rows = block // SIDE
    share = hid_hbm.shape[1]
    team = SIDE * SIDE
    last = sections - 1

    sec = lax.axis_index("section")
    me = lax.axis_index("tensor")
    my_z = me // SIDE
    my_y = me % SIDE

    def dev(s, t):
        return {"section": s, "tensor": t}

    loads = [pltpu.make_async_copy(wbc_hbm, w_all.at[:, pl.ds(0, n2)], load_sem.at[0])]
    for h in range(heads):
        loads.append(
            pltpu.make_async_copy(
                wzx_hbm.at[h], w_all.at[:, pl.ds(n2 + 128 * h, 128)], load_sem.at[1 + h]
            )
        )
    at = 1 + heads
    for yy in range(SIDE):
        loads.append(
            pltpu.make_async_copy(
                wout_hbm.at[:, pl.ds(chunk * yy, chunk)], w_o.at[yy], load_sem.at[at + yy]
            )
        )
    at += SIDE
    loads.append(pltpu.make_async_copy(ssm_hbm, st, load_sem.at[at]))
    smalls = [
        pltpu.make_async_copy(a, b, small_sem.at[i])
        for i, (a, b) in enumerate(
            (
                (wdt_hbm, wdt_ref),
                (gain_hbm, gain_ref),
                (dtb_hbm, dtb_ref),
                (alog_hbm, alog_ref),
                (dsk_hbm, dsk_ref),
                (cxw_hbm, cxw_ref),
                (cxb_hbm, cxb_ref),
                (cbw_hbm, cbw_ref),
                (cbb_hbm, cbb_ref),
                (ig_hbm, ig_ref),
                (cxs_hbm, cxs_ref),
                (cbs_hbm, cbs_ref),
            )
        )
    ]

    barrier = pltpu.get_barrier_semaphore()

    ring = [
        ((my_z + zo) % SIDE) * SIDE + (my_y + yo) % SIDE
        for yo, zo in sorted(
            ((yo, zo) for yo in FAR for zo in FAR),
            key=lambda o: sum(min(v, SIDE - v) for v in o),
            reverse=True,
        )
    ]

    for other in ring[:-1]:
        pl.semaphore_signal(barrier, inc=1, device_id=dev(sec, other), device_id_type=MESH)

    @pl.when(sec > 0)
    def _():
        for other in ring:
            pl.semaphore_signal(barrier, inc=1, device_id=dev(sec - 1, other), device_id_type=MESH)

    @pl.when(sec < last)
    def _():
        for other in ring:
            pl.semaphore_signal(barrier, inc=1, device_id=dev(sec + 1, other), device_id_type=MESH)

    hid_copy = pltpu.make_async_copy(hid_hbm, hid_ref, hid_sem)
    hid_copy.start()
    for cp in smalls + loads:
        cp.start()

    hid_copy.wait()
    for blk in range(BLOCKS):
        parts = [
            hid_ref[blk * block + rows * zz : blk * block + rows * zz + rows, :].astype(F32)
            if rows % 16 == 0
            else hid_ref[blk * block : blk * block + block, :].astype(F32)[rows * zz : rows * zz + rows]
            for zz in range(SIDE)
        ]
        pack[blk] = jnp.concatenate(parts, axis=1).astype(BF16)

    partners = team - 1 + jnp.where(sec > 0, team, 0) + jnp.where(sec < last, team, 0)
    pl.semaphore_wait(barrier, partners)

    def init_copy(blk, src_t, dest):
        return pltpu.make_async_remote_copy(
            src_ref=pack.at[blk],
            dst_ref=init_buf.at[blk, src_t],
            send_sem=init_send.at[blk, dest],
            recv_sem=init_recv.at[blk, src_t],
            device_id=dev(sec, dest),
            device_id_type=MESH,
        )

    def init_own(blk):
        return pltpu.make_async_copy(
            pack.at[blk], init_buf.at[blk, me], init_recv.at[blk, me]
        )

    @pl.when(sec == 0)
    def _():
        for blk in range(BLOCKS):
            for other in ring[:-1]:
                init_copy(blk, me, other).start()
            init_own(blk).start()

    for cp in smalls:
        cp.wait()
    wdt_pad[...] = jnp.zeros_like(wdt_pad)
    wdt_pad[0:heads, :] = wdt_ref[...].astype(F32)
    for h in range(1 + heads):
        loads[h].wait()
    for j in range(width // 128):
        blk = wdt_pad[:, 128 * j : 128 * j + 128]
        w_all[128 * j : 128 * j + 128, n2 + 128 * heads : n2 + 128 * heads + 128] = blk.T.astype(BF16)
    q_buf[...] = jnp.zeros_like(q_buf)
    cb_out[0] = cbs_ref[1]
    cb_out[1] = cbs_ref[2]
    cx_out[0] = cxs_ref[1]
    cx_out[1] = cxs_ref[2]
    cbw = cbw_ref[...]
    pre_bc[...] = (
        cbs_ref[0].astype(F32) * cbw[0:1]
        + cbs_ref[1].astype(F32) * cbw[1:2]
        + cbs_ref[2].astype(F32) * cbw[2:3]
        + cbb_ref[...]
    )
    pairs = (heads + 1) // 2

    def packed(get, k):
        a = get(2 * k)
        b = get(2 * k + 1) if 2 * k + 1 < heads else jnp.zeros_like(a)
        return jnp.concatenate([a, b], axis=1)

    def pre_of(h):
        w = cxw_ref[h]
        return (
            cxs_ref[0, h].astype(F32) * w[0:1]
            + cxs_ref[1, h].astype(F32) * w[1:2]
            + cxs_ref[2, h].astype(F32) * w[2:3]
            + cxb_ref[h]
        )

    for k in range(pairs):
        pre_x[k] = packed(pre_of, k)
        par[0, k] = packed(lambda h: cxw_ref[h][3:4], k)
        par[1, k] = packed(lambda h: ig_ref[h], k)
        par[2, k] = packed(
            lambda h: jnp.broadcast_to(dsk_ref[:, h : h + 1], (1, p_size)), k
        )
    pad = jnp.zeros((1, 128 - heads), F32)
    dtb = jnp.concatenate([dtb_ref[...], pad], axis=1)
    neg_a = -jnp.exp(jnp.concatenate([alog_ref[...], pad], axis=1))

    def ag_copy(blk, src_t, dest):
        return pltpu.make_async_remote_copy(
            src_ref=ag_src.at[blk],
            dst_ref=hbuf.at[blk, src_t % SIDE, src_t // SIDE],
            send_sem=ag_send.at[blk, dest],
            recv_sem=ag_recv.at[blk, src_t],
            device_id=dev(jnp.minimum(sec + 1, last), dest),
            device_id_type=MESH,
        )

    def rs_copy(blk, src_t, dest, yy, zz):
        return pltpu.make_async_remote_copy(
            src_ref=send_buf.at[blk, yy, zz],
            dst_ref=rs_buf.at[blk, src_t],
            send_sem=rs_send.at[blk, dest],
            recv_sem=rs_recv.at[blk, src_t],
            device_id=dev(sec, dest),
            device_id_type=MESH,
        )

    def rs_own(blk):
        return pltpu.make_async_copy(
            send_buf.at[blk, my_y, my_z], rs_buf.at[blk, me], rs_recv.at[blk, me]
        )

    def end_copy(blk, src_t, zz, j):
        return pltpu.make_async_remote_copy(
            src_ref=send_end.at[blk, zz, j],
            dst_ref=sum_end.at[blk, src_t],
            send_sem=rs_send.at[blk, zz * SIDE + j],
            recv_sem=rs_recv.at[blk, src_t],
            device_id=dev(sec, zz * SIDE + j),
            device_id_type=MESH,
        )

    def end_own(blk):
        return pltpu.make_async_copy(
            send_end.at[blk, my_z, my_y], sum_end.at[blk, me], rs_recv.at[blk, me]
        )

    for cp in loads[1 + heads :]:
        cp.wait()
    lane = lax.broadcasted_iota(jnp.int32, (block, 128), 1)
    low = lane < p_size
    hp = heads * p_size
    dt0 = n2 + 128 * heads
    group = 16
    row = lax.broadcasted_iota(jnp.int32, (group, n_state), 0)

    def layer(blk, carry):
        here = pl.ds(pl.multiple_of(blk * block, block), block)

        @pl.when(sec == 0)
        def _():
            for other in ring[:-1]:
                init_copy(blk, other, me).wait_recv()
            init_own(blk).wait()
            for yy in range(SIDE):
                parts = [init_buf[blk, SIDE * yy + i].astype(F32) for i in range(SIDE)]
                for zz in range(SIDE):
                    hbuf[blk, yy, zz] = jnp.concatenate(
                        [part[:, share * zz : share * zz + share] for part in parts], axis=1
                    ).astype(BF16)

        sq = jnp.zeros((block, 128), F32)
        for off in NEAR:
            yy = (my_y + off) % SIDE

            @pl.when(sec > 0)
            def _():
                for zo in NEAR:
                    ag_copy(blk, ((my_z + zo) % SIDE) * SIDE + yy, me).wait_recv()

            hv = jnp.concatenate([hbuf[blk, yy, zz].astype(F32) for zz in range(SIDE)], axis=0)
            for i in range(chunk // 128):
                part = hv[:, 128 * i : 128 * i + 128]
                sq = sq + part * part
            start = pl.multiple_of(yy * chunk, chunk)
            hg = (hv * gain_ref[:, pl.ds(start, chunk)]).astype(BF16)
            term = jnp.dot(hg, w_all[pl.ds(start, chunk), :], preferred_element_type=F32)
            if off == NEAR[0]:
                acc[...] = term
            else:
                acc[...] += term
        r = lax.rsqrt(jnp.sum(sq, axis=1, keepdims=True) * (1.0 / width) + epsilon)

        bcf = (acc[:, 0:n2] * r).astype(BF16)
        cb_out[2, here, :] = bcf
        bcv = silu(pre_bc[here, :] + bcf.astype(F32) * cbw_ref[3:4, :])
        b_in = bcv[:, 0:n_state]
        c_out = bcv[:, n_state:n2]
        b_buf[here, :] = b_in
        bd = jnp.sum(b_in * c_out, axis=1, keepdims=True)

        for g in range(block // group):
            c16 = c_out[group * g : group * g + group]
            base = blk * block + group * g
            total = None
            for i in range(0, group, 2):
                lhs = jnp.concatenate(
                    [jnp.where(row == i, c16, 0.0), jnp.where(row == i + 1, c16, 0.0)], axis=1
                ).astype(BF16)
                rhs = jnp.concatenate([st[base + i], st[base + i + 1]], axis=1)
                term = lax.dot_general(
                    lhs, rhs, (((1,), (1,)), ((), ())), preferred_element_type=F32
                )
                total = term if total is None else total + term
            q_buf[group * g : group * g + group, 0:hp] = total

        step = softplus(acc[:, dt0 : dt0 + 128] * r + dtb)
        decay = jnp.exp(step * neg_a)

        def each(v):
            return [jnp.broadcast_to(v[:, h : h + 1], (block, 128)) for h in range(heads)]

        steps, decays = each(step), each(decay)
        for h in range(heads):
            dec[h, here, :] = decays[h]

        def spread(v, k):
            return jnp.where(low, v[2 * k], v[min(2 * k + 1, heads - 1)])

        sq = jnp.zeros((block, 128), F32)
        for k in range(pairs):
            a = acc[:, n2 + 256 * k : n2 + 256 * k + 128]
            if 2 * k + 1 < heads:
                b = acc[:, n2 + 256 * k + 128 : n2 + 256 * k + 256]
            else:
                b = jnp.zeros_like(a)
            x_new = jnp.where(low, pltpu.roll(a, p_size, 1), b)
            z_new = jnp.where(low, a, pltpu.roll(b, p_size, 1))
            xf = (x_new * r).astype(BF16)
            xf_buf[k, here, :] = xf
            xc = silu(pre_x[k, here, :] + xf.astype(F32) * par[0, k])
            sx = spread(steps, k) * xc
            stx[k, here, :] = sx
            q = q_buf[:, 128 * k : 128 * k + 128]
            y_out = spread(decays, k) * q + sx * bd + par[2, k] * xc
            gated = y_out * silu(z_new * r)
            sq = sq + gated * gated
            inner[:, 128 * k : 128 * k + 128] = (gated * par[1, k]).astype(BF16)
        squares = jnp.sum(sq, axis=1, keepdims=True)
        hi = squares.astype(BF16).astype(F32)
        lo = squares - hi
        sq_tile = jnp.where(lane == 0, hi, jnp.where(lane == 1, lo, 0.0))

        for yo in FAR:
            yy = (jnp.where(sec < last, my_y, my_z) + yo) % SIDE
            part = jnp.dot(inner[:, 0:hp], w_o[yy], preferred_element_type=F32)

            @pl.when(sec < last)
            def _():
                whole = jnp.concatenate([part, sq_tile], axis=1)
                for zz in range(SIDE):
                    send_buf[blk, yy, zz] = whole[rows * zz : rows * zz + rows].astype(BF16)
                for zo in FAR:
                    zz = (my_z + zo) % SIDE
                    if yo == 0 and zo == 0:
                        rs_own(blk).start()
                    else:
                        rs_copy(blk, me, zz * SIDE + yy, yy, zz).start()

            @pl.when(sec == last)
            def _():
                for j in range(SIDE):
                    send_end[blk, yy, j] = jnp.concatenate(
                        [part[:, 128 * j : 128 * j + 256], sq_tile], axis=1
                    ).astype(BF16)
                for jo in FAR:
                    j = (my_y + jo) % SIDE
                    if yo == 0 and jo == 0:
                        end_own(blk).start()
                    else:
                        end_copy(blk, me, yy, j).start()

        return carry

    lax.fori_loop(0, BLOCKS, layer, 0)

    octet = 8
    per_block = block // octet

    def turn():
        zeros = jnp.zeros((128 - streams, 128), F32)
        for k in range(pairs):
            turned = jnp.concatenate([stx[k], zeros], axis=0).T
            stx_t[128 * k : 128 * k + 128] = turned[:, 0:streams].astype(BF16)

    at_stream = lax.broadcasted_iota(jnp.int32, (streams, n_state), 0)

    def update(g, carry):
        span8 = pl.ds(pl.multiple_of(g * octet, octet), octet)
        b8 = b_buf[span8, :]
        for i in range(0, octet, 2):
            rhs = jnp.concatenate(
                [jnp.where(at_stream == g * octet + i + e, b8[i + e : i + e + 1], 0.0) for e in (0, 1)],
                axis=1,
            ).astype(BF16)
            more = jnp.dot(stx_t[0:hp, :], rhs, preferred_element_type=F32)
            for e in (0, 1):
                for h in range(heads):
                    span = slice(p_size * h, p_size * h + p_size)
                    old = st[g * octet + i + e, span, :].astype(F32)
                    new = (
                        dec[h, span8, :][i + e : i + e + 1] * old
                        + more[span, n_state * e : n_state * e + n_state]
                    )
                    st[g * octet + i + e, span, :] = new.astype(BF16)
        return carry

    def sh_copy(blk, src_z, j):
        return pltpu.make_async_remote_copy(
            src_ref=ag_src.at[blk],
            dst_ref=sh_buf.at[blk, src_z],
            send_sem=sh_send.at[blk, j],
            recv_sem=sh_recv.at[blk, src_z],
            device_id=dev(sec, my_y * SIDE + j),
            device_id_type=MESH,
        )

    @pl.when(sec == last)
    def _():
        turn()

    for blk in range(BLOCKS):
        lax.fori_loop(
            EARLY[blk - 1] if blk else 0,
            jnp.where(sec == last, EARLY[blk], EARLY[blk - 1] if blk else 0),
            update,
            0,
        )

        @pl.when(sec < last)
        def _():
            tot = jnp.zeros((rows, chunk + 128), F32)
            for i, src in enumerate(reversed(ring)):
                if i == 0:
                    rs_own(blk).wait()
                else:
                    rs_copy(blk, src, me, my_y, my_z).wait_recv()
                tot = tot + rs_buf[blk, src].astype(F32)
            scale = lax.rsqrt(
                jnp.sum(tot[:, chunk : chunk + 128], axis=1, keepdims=True) * (1.0 / (hp * team))
                + epsilon
            )
            mine = hbuf[blk, my_y, my_z].astype(F32)
            ag_src[blk] = (mine + tot[:, 0:chunk] * scale).astype(BF16)

            for other in ring:
                ag_copy(blk, me, other).start()

        @pl.when(sec == last)
        def _():
            tot = jnp.zeros((block, 384), F32)
            for i, src in enumerate(reversed(ring)):
                if i == 0:
                    end_own(blk).wait()
                else:
                    end_copy(blk, src, my_z, my_y).wait_recv()
                tot = tot + sum_end[blk, src].astype(F32)
            scale = lax.rsqrt(
                jnp.sum(tot[:, 256:384], axis=1, keepdims=True) * (1.0 / (hp * team)) + epsilon
            )
            window = pl.ds(pl.multiple_of(my_y * 128, 128), 256)
            mine = jnp.concatenate(
                [hbuf[blk, my_z, zz, :, window].astype(F32) for zz in range(SIDE)], axis=0
            )
            end_buf[...] = mine + tot[:, 0:256] * scale
            for j in range(SIDE):

                @pl.when(my_y == j)
                def _():
                    first = (share - 128) * j
                    sec_out[blk * block : blk * block + block, :] = end_buf[...][
                        :, first : first + share
                    ].astype(BF16)

    @pl.when(sec < last)
    def _():
        for blk in range(BLOCKS):
            for j in range(SIDE):
                own = my_y * SIDE + j == me

                @pl.when(own)
                def _():
                    pltpu.make_async_copy(
                        ag_src.at[blk], sh_buf.at[blk, my_z], sh_recv.at[blk, my_z]
                    ).start()

                @pl.when(jnp.logical_not(own))
                def _():
                    sh_copy(blk, my_z, j).start()

    @pl.when(sec < last)
    def _():
        turn()

    lax.fori_loop(jnp.where(sec == last, EARLY[-1], 0), streams // octet, update, 0)

    for h in range(heads):
        xf = xf_buf[h // 2].astype(F32)
        cx_out[2, h] = xf[:, p_size * (h % 2) : p_size * (h % 2) + p_size].astype(BF16)

    @pl.when(sec < last)
    def _():
        for blk in range(BLOCKS):
            for zz in range(SIDE):
                sh_copy(blk, zz, 0).wait_recv()
        for yy in range(SIDE):

            @pl.when(my_y == yy)
            def _():
                whole = jnp.concatenate(
                    [
                        sh_buf[blk, zz].astype(F32)
                        for blk in range(BLOCKS)
                        for zz in range(SIDE)
                    ],
                    axis=0,
                )
                sec_out[...] = whole[:, share * yy : share * yy + share].astype(BF16)

    @pl.when(sec < last)
    def _():
        for blk in range(BLOCKS):
            for other in ring[:-1]:
                rs_copy(blk, me, other, my_y, my_z).wait_send()
            for dest in range(team):
                ag_copy(blk, me, dest).wait_send()
            for j in range(SIDE):

                @pl.when(my_y * SIDE + j != me)
                def _():
                    sh_copy(blk, my_z, j).wait_send()

    @pl.when(sec == last)
    def _():
        for blk in range(BLOCKS):
            for other in ring[:-1]:
                end_copy(blk, me, other // SIDE, other % SIDE).wait_send()

    @pl.when(sec == 0)
    def _():
        for blk in range(BLOCKS):
            for other in ring[:-1]:
                init_copy(blk, me, other).wait_send()


def write_out(a_in, b_in, c_in, d_in, a_out, b_out, c_out, d_out, sems):
    size = d_in.shape[0] // PIECES
    copies = [
        pltpu.make_async_copy(d_in.at[pl.ds(size * i, size)], d_out.at[pl.ds(size * i, size)], sems.at[3 + i])
        for i in range(PIECES)
    ]
    for i, (x, y) in enumerate(((a_in, a_out), (b_in, b_out), (c_in, c_out))):
        copies.append(pltpu.make_async_copy(x, y, sems.at[i]))
    for cp in copies:
        cp.start()
    for cp in copies:
        cp.wait()


def shards(
    hidden_in,
    pre_gain,
    w_zx,
    w_bc,
    w_dt,
    dt_bias,
    a_log,
    d_skip,
    conv_x_weight,
    conv_x_bias,
    conv_bc_weight,
    conv_bc_bias,
    inner_gain,
    w_out,
    conv_x_state,
    conv_bc_state,
    ssm_state,
    sections,
):
    streams, share = hidden_in.shape
    _, heads, p_size, width = w_out.shape
    n2 = w_bc.shape[2]
    n_state = n2 // 2
    team = SIDE * SIDE
    chunk, block = width // SIDE, streams // BLOCKS
    rows = block // SIDE
    hp = heads * p_size
    cols = n2 + 128 * heads + 128
    pairs = (heads + 1) // 2
    args = (
        hidden_in,
        pre_gain,
        jnp.transpose(w_zx[0], (1, 0, 2)),
        w_bc[0],
        jnp.transpose(w_dt[0], (1, 0)),
        dt_bias,
        a_log,
        d_skip,
        jnp.transpose(conv_x_weight[0], (1, 0, 2)),
        jnp.transpose(conv_x_bias, (1, 0, 2)),
        conv_bc_weight[0],
        conv_bc_bias,
        jnp.transpose(inner_gain, (1, 0, 2)),
        w_out[0].reshape(hp, width),
        jnp.transpose(conv_x_state[0], (1, 2, 0, 3)),
        jnp.transpose(conv_bc_state[0], (1, 0, 2)),
        ssm_state[0].reshape(streams, hp, n_state),
    )
    vmem = pl.BlockSpec(memory_space=pltpu.VMEM)
    hbm = pl.BlockSpec(memory_space=pltpu.HBM)
    small = (1, 4, 5, 6, 7, 8, 9, 10, 11, 12, 14, 15)
    dma = pltpu.SemaphoreType.DMA
    sec_new, cx_new, cb_new, ssm_new = pl.pallas_call(
        functools.partial(kernel, sections),
        out_shape=(
            jax.ShapeDtypeStruct((streams, share), BF16),
            jax.ShapeDtypeStruct((3, heads, streams, p_size), BF16),
            jax.ShapeDtypeStruct((3, streams, n2), BF16),
            jax.ShapeDtypeStruct((streams, hp, n_state), BF16),
        ),
        in_specs=[hbm] * len(args),
        out_specs=(vmem, vmem, vmem, vmem),
        scratch_shapes=[
            pltpu.VMEM((streams, share), BF16),
            pltpu.VMEM((BLOCKS, rows, chunk), BF16),
        ]
        + [pltpu.VMEM(args[i].shape, args[i].dtype) for i in small]
        + [
            pltpu.VMEM((width, cols), BF16),
            pltpu.VMEM((SIDE, hp, chunk), BF16),
            pltpu.VMEM((BLOCKS, SIDE, SIDE, rows, chunk), BF16),
            pltpu.VMEM((block, cols), F32),
            pltpu.VMEM((128, width), F32),
            pltpu.VMEM((streams, n2), F32),
            pltpu.VMEM((pairs, streams, 128), F32),
            pltpu.VMEM((3, pairs, 1, 128), F32),
            pltpu.VMEM((block, 128 * pairs), F32),
            pltpu.VMEM((block, 128 * pairs), BF16),
            pltpu.VMEM((pairs, streams, 128), F32),
            pltpu.VMEM((heads, streams, 128), F32),
            pltpu.VMEM((streams, n_state), F32),
            pltpu.VMEM((pairs, streams, 128), BF16),
            pltpu.VMEM((128 * pairs, streams), BF16),
            pltpu.VMEM((BLOCKS, SIDE, SIDE, rows, chunk + 128), BF16),
            pltpu.VMEM((BLOCKS, team, rows, chunk + 128), BF16),
            pltpu.VMEM((BLOCKS, rows, chunk), BF16),
            pltpu.VMEM((BLOCKS, team, rows, chunk), BF16),
            pltpu.VMEM((BLOCKS, SIDE, rows, chunk), BF16),
            pltpu.VMEM((BLOCKS, SIDE, SIDE, block, 384), BF16),
            pltpu.VMEM((BLOCKS, team, block, 384), BF16),
            pltpu.VMEM((block, 256), F32),
            dma(()),
            dma((1 + heads + SIDE + 1,)),
            dma((len(small),)),
            dma((BLOCKS, team)),
            dma((BLOCKS, team)),
            dma((BLOCKS, team)),
            dma((BLOCKS, team)),
            dma((BLOCKS, team)),
            dma((BLOCKS, team)),
            dma((BLOCKS, SIDE)),
            dma((BLOCKS, SIDE)),
        ],
        compiler_params=pltpu.CompilerParams(
            collective_id=0, has_side_effects=True, vmem_limit_bytes=40 * 1024 * 1024
        ),
        name="stack_step",
    )(*[pltpu.with_memory_space_constraint(a, pltpu.HBM) for a in args])
    results = (sec_new, cx_new, cb_new, ssm_new)
    sec_new, cx_new, cb_new, ssm_new = pl.pallas_call(
        write_out,
        out_shape=tuple(jax.ShapeDtypeStruct(a.shape, a.dtype) for a in results),
        in_specs=[vmem] * 4,
        out_specs=(pl.BlockSpec(memory_space=pltpu.HBM),) * 4,
        scratch_shapes=[dma((3 + PIECES,))],
        compiler_params=pltpu.CompilerParams(vmem_limit_bytes=16 * 1024 * 1024),
        name="write_out",
    )(*results)
    return (
        sec_new[None],
        jnp.transpose(cx_new, (2, 0, 1, 3))[None],
        jnp.transpose(cb_new, (1, 0, 2))[None],
        ssm_new.reshape(ssm_state.shape),
    )


def solution(mesh):
    placed = (
        P(None, "tensor"),
        P("section", None),
        P("section", None, "tensor", None),
        P("section", None, None),
        P("section", None, "tensor"),
        P("section", "tensor"),
        P("section", "tensor"),
        P("section", "tensor"),
        P("section", None, "tensor", None),
        P("section", "tensor", None),
        P("section", None, None),
        P("section", None),
        P("section", "tensor", None),
        P("section", "tensor", None, None),
        P("section", None, None, "tensor", None),
        P("section", None, None, None),
        P("section", None, "tensor", None, None),
    )
    return jax.shard_map(
        functools.partial(shards, sections=mesh.shape["section"]),
        mesh=mesh,
        in_specs=placed,
        out_specs=(
            P("section", None, "tensor"),
            P("section", None, None, "tensor", None),
            P("section", None, None, None),
            P("section", None, "tensor", None, None),
        ),
        check_vma=False,
    )
```
